32 devices in a mesh: groups: 2 (over y), ctx: 4 (over z), section: 2 (over x), mp: 2 (over core).
Axes of the slice: x: 2, y: 2, z: 4, core: 2. Of those that a mesh axis runs over, the one named last changes fastest.
Arguments:
- spans: bfloat16 [2, 1024, 6144], P('section', ('groups', 'ctx'), 'mp'), parts along dimension 1, may hold values from -6 to 6
- norm_gain: float32 [2, 6144], P('section', 'mp'), may hold values from 0.25 to 1.75
- w_in: bfloat16 [2, 6144, 3, 4096], P('section', 'mp', None, 'ctx'), may hold values from -0.078125 to 0.078125
- filters: bfloat16 [2, 4096, 128], P('section', 'ctx'), may hold values from -0.5 to 0.5
- w_out: bfloat16 [2, 4096, 6144], P('section', 'ctx', 'mp'), may hold values from -0.09375 to 0.09375
- prompt_len: int32 [4], P(('groups', 'section')), parts along dimension 0, may hold values from 128 to 512
- needles: int32 [2, 128], P('section', 'groups'), parts along dimension 1, may hold values from 0 to 511
Outputs:
- advanced: bfloat16 [2, 1024, 6144], P('section', ('groups', 'ctx'), 'mp'), parts along dimension 1
- needle_states: bfloat16 [2, 128, 4096], P('section', 'groups', 'ctx'), parts along dimension 1
The draws below stay inside these ranges and needn't reach their ends.
There are 2 independent parts, one for each index of `groups`. The reference program is written for one: setup_inputs(seed, part) draws one part's arguments, and reference() takes and returns one part's arrays. A program takes and returns all parts, laid end to end along the dimension named above; an argument that names none is the same for every part. Nothing has to cross between parts.
All inputs are finite; a program needn't handle non-finite values.
Results may differ from the reference program's by a relative error of at most 0.02.
Values may be sent and summed in bfloat16 or wider, within the bound.
No kernel may reach another device: no remote copies, remote signals or barrier semaphores. Data moves between devices by JAX's collectives and lax.ppermute only.
A program may use at most 256 MiB of HBM per device.

```python
import jax
import jax.numpy as jnp
from jax import lax

D = 6144
C = 4096
TAPS = 128
NEEDLES = 64
TOKENS = 512
SECTIONS = 2
N_CTX = 4
N_SECTION = 2


def touch_ends(array, own_key, smallest, high):
    place = [jax.random.randint(jax.random.fold_in(own_key, axis), (), 0, length) for axis, length in enumerate(array.shape)]
    longest = array.shape.index(max(array.shape))
    beside = place[:longest] + [(place[longest] + 1) % array.shape[longest]] + place[longest + 1:]
    return array.at[tuple(place)].set(smallest).at[tuple(beside)].set(high)


def shard_levels(rng, extent, pieces, least, high):
    def one(position, blocks):
        heights = jax.random.uniform(jax.random.fold_in(jax.random.fold_in(rng, 6), position), (blocks,), jnp.float32, least / len(pieces), high / len(pieces))
        return jnp.repeat(jnp.exp(heights), extent[position] // blocks).reshape((-1,) + (1,) * (len(extent) - position - 1))

    loudness = one(*pieces[0])
    for cut in pieces[1:]:
        loudness = loudness * one(*cut)
    return loudness


def centred(key, extent, scale, reach, shards=(), dtype=jnp.bfloat16):
    level = shard_levels(key, extent, shards, -0.22, 0.18) if shards else 1.0
    entries = jax.random.normal(key, extent, jnp.float32) * scale * level
    return jnp.minimum(jnp.maximum(entries, -reach), reach).astype(dtype)


def setup_inputs(seed: int = 0, part: int = 0) -> dict:
    seeds = jax.random.split(jax.random.key(seed), 8)
    part_splits = jax.random.split(jax.random.fold_in(seeds[7], part), 8)
    return {
        "spans": centred(part_splits[0], (SECTIONS, TOKENS, D), 1.0, 6.0, ((0, 2), (1, 4), (2, 2))),
        "norm_gain": jnp.clip(1.0 + 0.15 * jax.random.normal(seeds[1], (SECTIONS, D), jnp.float32), 0.25, 1.75),
        "w_in": centred(seeds[2], (SECTIONS, D, 3, C), D ** -0.5, 0.078125, ((0, 2), (1, 2), (3, 4))),
        "filters": centred(seeds[3], (SECTIONS, C, TAPS), TAPS ** -0.5, 0.5, ((0, 2), (1, 4))),
        "w_out": centred(seeds[4], (SECTIONS, C, D), C ** -0.5, 0.09375, ((0, 2), (1, 4), (2, 2))),
        "prompt_len": jax.random.randint(part_splits[5], (SECTIONS,), TOKENS // 4, TOKENS + 1).astype(jnp.int32),
        "needles": touch_ends(jax.random.randint(part_splits[6], (SECTIONS, NEEDLES), 0, TOKENS), jax.random.fold_in(part_splits[6], 1), 0, TOKENS - 1).astype(jnp.int32),
    }


norm_eps = 1e-06

def reference(spans, norm_gain, w_in, filters, w_out, prompt_len, needles):
    results = []
    picked_all = []
    block = C // N_CTX
    for section_id in range(N_SECTION):
        xval = spans[section_id].astype(jnp.float32)
        mean_sq = lax.optimization_barrier(jnp.mean(xval * xval, axis=1, keepdims=True))
        scaled = (xval * norm_gain[section_id][None, :]).astype(jnp.bfloat16)
        proj = jnp.dot(scaled, w_in[section_id].reshape(D, 3 * C), preferred_element_type=jnp.float32).reshape(TOKENS, 3, C)
        proj = proj * lax.rsqrt(mean_sq + norm_eps)[:, :, None]
        live = (jnp.arange(TOKENS) < prompt_len[section_id]).astype(jnp.float32)[:, None]
        mixed = (proj[:, 1] * proj[:, 2] * live).astype(jnp.bfloat16).astype(jnp.float32)
        padded = jnp.concatenate([jnp.zeros((TAPS, C), jnp.float32), mixed], axis=0)
        filt = filters[section_id].astype(jnp.float32)

        def conv_step(index, accum):
            shifted = lax.dynamic_slice_in_dim(padded, TAPS - index, TOKENS, 0)
            tap_col = lax.dynamic_slice_in_dim(filt, index, 1, 1)[:, 0]
            return accum + shifted * tap_col[None, :]
        conv = lax.fori_loop(0, TAPS, conv_step, jnp.zeros((TOKENS, C), jnp.float32))
        gated = (proj[:, 0] * conv * live).astype(jnp.bfloat16)
        picked_all.append(gated[needles[section_id]])
        total = jnp.zeros((TOKENS, D), jnp.float32)
        for blk in range(N_CTX):
            part = jnp.dot(gated[:, blk * block:(blk + 1) * block], w_out[section_id][blk * block:(blk + 1) * block], preferred_element_type=jnp.float32)
            part = lax.optimization_barrier(part.astype(jnp.bfloat16)).astype(jnp.float32)
            total = total + part
        results.append((xval + total).astype(jnp.bfloat16))
    advanced = jnp.roll(jnp.stack(results), 1, axis=0)
    return (advanced, jnp.stack(picked_all))
```

```python
import functools

import jax
import jax.numpy as jnp
from jax import lax
from jax.experimental import pallas as pl
from jax.experimental.pallas import tpu as pltpu
from jax.sharding import PartitionSpec as P

norm_eps = 1e-06
lanes = 128
sublanes = 8
halves = 2
vmem_limit = 40 * 1024 * 1024


def tile_of(extent, most):
    tile = min(extent, most)
    while extent % tile:
        tile //= 2
    return tile


def smem():
    return pl.BlockSpec(memory_space=pltpu.SMEM)


def params():
    return pltpu.CompilerParams(vmem_limit_bytes=vmem_limit)


def project_kernel(merged, parts, line, table_ref, gain_ref, *refs):
    step = pl.program_id(0)
    x_refs = refs[:parts]
    w_ref, out_ref, scaled, stat = refs[parts:]
    tile = out_ref.shape[1]
    busy = table_ref[line, 4] > 0
    last = step == pl.num_programs(0) - 1

    @pl.when(busy & (step == 0))
    def _():
        half = parts // 2
        chunk = x_refs[0].shape[0]
        for index in range(half if merged else parts):
            x = x_refs[index][...].astype(jnp.float32)
            if merged:
                x = x + x_refs[half + index][...].astype(jnp.float32)
            place = slice(index * chunk, (index + 1) * chunk)
            scaled[place, :] = (x * gain_ref[...]).astype(jnp.bfloat16)
            squares = jnp.sum(x * x, axis=1, keepdims=True)
            high = squares.astype(jnp.bfloat16).astype(jnp.float32)
            low = squares - high
            column = lax.broadcasted_iota(jnp.int32, (chunk, tile), 1)
            stat[place, :] = jnp.where(column == 0, high, jnp.where(column == 1, low, 0.0)).astype(jnp.bfloat16)

    @pl.when(busy & jnp.logical_not(last))
    def _():
        out_ref[...] = jnp.dot(scaled[...], w_ref[0], preferred_element_type=jnp.float32).astype(jnp.bfloat16)

    @pl.when(busy & last)
    def _():
        out_ref[...] = stat[...]

    @pl.when(jnp.logical_not(busy))
    def _():
        out_ref[...] = jnp.zeros_like(out_ref)


def project(pieces, merged, table, line, gain, w):
    streams, depth, channels = w.shape
    chunk = pieces[0].shape[0]
    rows = chunk * (len(pieces) // 2 if merged else len(pieces))
    tile = tile_of(channels, 256)
    per = channels // tile
    steps = streams * per
    whole = pl.BlockSpec((chunk, depth), lambda i: (0, 0))

    def weights(i):
        j = jnp.minimum(i, steps - 1)
        return (j // per, 0, j % per)

    return pl.pallas_call(
        functools.partial(project_kernel, merged, len(pieces), line),
        grid=(steps + 1,),
        in_specs=[smem(), pl.BlockSpec((1, depth), lambda i: (0, 0))]
        + [whole] * len(pieces)
        + [pl.BlockSpec((1, depth, tile), weights)],
        out_specs=pl.BlockSpec((rows, tile), lambda i: (0, i)),
        out_shape=jax.ShapeDtypeStruct((rows, streams * channels + tile), jnp.bfloat16),
        scratch_shapes=[pltpu.VMEM((rows, depth), jnp.bfloat16), pltpu.VMEM((rows, tile), jnp.bfloat16)],
        compiler_params=params(),
        cost_estimate=pl.CostEstimate(
            flops=2 * rows * depth * streams * channels,
            bytes_accessed=2 * streams * depth * channels,
            transcendentals=0,
        ),
        name="project",
    )(table, gain, *pieces, w)


def mix_kernel(full_width, line, table_ref, *refs):
    q0, k0, v0, s0, q1, k1, v1, s1, pk0, pv0, ps0, pk1, pv1, ps1, f_ref, out_ref, window, turned = refs
    rows = out_ref.shape[0]
    taps = f_ref.shape[0]
    block = table_ref[line, 0]
    length = table_ref[line, 1]
    work = table_ref[line, 2] > 0

    def joined(a_ref, b_ref):
        return a_ref[...].astype(jnp.float32) + b_ref[...].astype(jnp.float32)

    def inverse(a_ref, b_ref):
        mean = jnp.sum(joined(a_ref, b_ref), axis=1, keepdims=True) / full_width
        return lax.rsqrt(mean + norm_eps)

    @pl.when(work)
    def _():
        row = lax.broadcasted_iota(jnp.int32, (rows, 1), 0)
        scale = inverse(s0, s1)
        live = (row + block * rows < length).astype(jnp.float32)
        here = joined(k0, k1) * scale * (joined(v0, v1) * scale) * live
        window[rows:, :] = here.astype(jnp.bfloat16).astype(jnp.float32)

        @pl.when(table_ref[line, 3] > 0)
        def _():
            scale = inverse(ps0, ps1)
            live = (row + (block - 1) * rows < length).astype(jnp.float32)
            before = joined(pk0, pk1) * scale * (joined(pv0, pv1) * scale) * live
            window[:rows, :] = before.astype(jnp.bfloat16).astype(jnp.float32)

        @pl.when(table_ref[line, 3] == 0)
        def _():
            window[:rows, :] = jnp.zeros((rows, window.shape[1]), jnp.float32)

        total = jnp.zeros((rows, out_ref.shape[1]), jnp.float32)
        for shift in range(sublanes):
            rolled = pltpu.roll(window[...], shift, 0) if shift else window[...]
            for group in range(taps // sublanes):
                tap = group * sublanes + shift
                start = rows - group * sublanes
                total = total + rolled[start : start + rows, :] * f_ref[tap : tap + 1, :]
        out_ref[...] = (joined(q0, q1) * scale * total * live).astype(jnp.bfloat16)

    @pl.when(jnp.logical_not(work))
    def _():
        out_ref[...] = jnp.zeros_like(out_ref)


def mix(table, line, here, before, rows, taps_first, full_width):
    own, got, at = here
    own_before, got_before, at_before = before
    taps, channels = taps_first.shape
    per = channels // lanes
    streams = 3

    def spec(at, stream):
        return pl.BlockSpec((rows, lanes), lambda i: (at, stream * per + i))

    def stat(at):
        return pl.BlockSpec((rows, lanes), lambda i: (at, streams * per))

    return pl.pallas_call(
        functools.partial(mix_kernel, full_width, line),
        grid=(per,),
        in_specs=[smem()]
        + [spec(at, 0), spec(at, 1), spec(at, 2), stat(at)] * 2
        + [spec(at_before, 1), spec(at_before, 2), stat(at_before)] * 2
        + [pl.BlockSpec((taps, lanes), lambda i: (0, i))],
        out_specs=pl.BlockSpec((rows, lanes), lambda i: (0, i)),
        out_shape=jax.ShapeDtypeStruct((rows, channels), jnp.bfloat16),
        scratch_shapes=[pltpu.VMEM((2 * rows, lanes), jnp.float32), pltpu.VMEM((2 * rows, lanes), jnp.float32)],
        compiler_params=params(),
        cost_estimate=pl.CostEstimate(
            flops=2 * rows * taps * channels, bytes_accessed=32 * rows * channels, transcendentals=0
        ),
        name="mix",
    )(table, own, own, own, own, got, got, got, got, own_before, own_before, own_before, got_before, got_before, got_before, taps_first)


def emit_kernel(line, table_ref, gated_ref, w_ref, *out_refs):
    work = table_ref[line, 2] > 0
    chunk = out_refs[0].shape[0]

    @pl.when(work)
    def _():
        product = jnp.dot(gated_ref[...], w_ref[...], preferred_element_type=jnp.float32).astype(jnp.bfloat16)
        for index, out_ref in enumerate(out_refs):
            out_ref[...] = product[index * chunk : (index + 1) * chunk, :]

    @pl.when(jnp.logical_not(work))
    def _():
        for out_ref in out_refs:
            out_ref[...] = jnp.zeros_like(out_ref)


def emit(table, line, gated, w):
    rows, channels = gated.shape
    width = w.shape[1]
    tile = tile_of(width, 512)
    chunk = rows // halves
    return pl.pallas_call(
        functools.partial(emit_kernel, line),
        grid=(width // tile,),
        in_specs=[
            smem(),
            pl.BlockSpec((rows, channels), lambda i: (0, 0)),
            pl.BlockSpec((channels, tile), lambda i: (0, i)),
        ],
        out_specs=[pl.BlockSpec((chunk, tile), lambda i: (0, i))] * halves,
        out_shape=[jax.ShapeDtypeStruct((chunk, width), jnp.bfloat16)] * halves,
        compiler_params=params(),
        cost_estimate=pl.CostEstimate(
            flops=2 * rows * channels * width, bytes_accessed=2 * channels * width, transcendentals=0
        ),
        name="emit",
    )(table, gated, w)


def added(*terms):
    total = terms[0].astype(jnp.float32)
    for term in terms[1:]:
        total = total + term.astype(jnp.float32)
    return total.astype(jnp.bfloat16)


def on_device(spans, norm_gain, w_in, filters, w_out, prompt_len, needles):
    count = lax.axis_size("ctx")
    place = lax.axis_index("ctx")
    x_local = spans[0]
    rows, half_width = x_local.shape
    chunk = rows // halves
    full_width = half_width * lax.axis_size("mp")
    weights = jnp.swapaxes(w_in[0], 0, 1)
    taps_first = filters[0].T.astype(jnp.float32)
    gain = norm_gain
    up = [(source, source + 1) for source in range(count - 1)]
    down = [(source + 1, source) for source in range(count - 1)]
    partner = [(0, 1), (1, 0)] if lax.axis_size("mp") == 2 else None

    order = [("d", 0)] + [(kind, k) for k in range(1, count) for kind in "du"]
    offsets = jnp.array([k if kind == "d" else -k for kind, k in order], jnp.int32)
    blocks = place.astype(jnp.int32) + offsets
    work = (blocks >= 0) & (blocks < count)
    busy = work | jnp.concatenate([work[:1], jnp.roll(work[1:].reshape(-1, 2), 1, axis=1).reshape(-1)])
    table = jnp.stack(
        [blocks, jnp.broadcast_to(prompt_len[0], blocks.shape), work, (blocks >= 1) & work, busy], axis=1
    ).astype(jnp.int32)
    line = {slot: index for index, slot in enumerate(order)}

    pieces = [x_local[i * chunk : (i + 1) * chunk] for i in range(halves)]
    gathered = {("d", 0): pieces, ("u", 0): pieces}
    for k in range(1, count):
        ups = [lax.ppermute(v, "ctx", [(a, b) for a, b in up if a >= k - 1]) for v in gathered["u", k - 1]]
        downs = [lax.ppermute(v, "ctx", [(a, b) for a, b in down if a <= count - k]) for v in gathered["d", k - 1]]
        gathered["u", k] = ups
        gathered["d", k] = downs

    held = {}
    for k in range(count):
        merged = 2 * k >= count
        if k == 0:
            own = project(pieces, False, table, 0, gain, weights)
        else:
            own = project(gathered["u", k] + gathered["d", k], merged, table, line["d", k], gain, weights)
        got = lax.ppermute(own, "mp", partner)
        held["u", k] = (own, got, 0)
        held["d", k] = (own, got, 0 if merged or k == 0 else 1)

    gated = {}

    def blend(kind, k):
        before = ("d", k - 1) if kind == "d" and k else ("u", k + 1)
        if before not in held:
            before = (kind, k)
        gated[kind, k] = mix(table, line[kind, k], held[kind, k], held[before], rows, taps_first, full_width)
        return emit(table, line[kind, k], gated[kind, k], w_out[0])

    sums = {}
    for k in range(count - 1, 0, -1):
        for kind in "du":
            sums[kind, k] = blend(kind, k)
    sums["d", 0] = blend("d", 0)

    for k in range(count - 1, 0, -1):
        arrived_up = [lax.ppermute(v, "ctx", [(a, b) for a, b in up if a + k <= count - 1]) for v in sums["d", k]]
        arrived_down = [lax.ppermute(v, "ctx", [(a, b) for a, b in down if a >= k]) for v in sums["u", k]]
        if k > 1:
            sums["d", k - 1] = [added(a, b) for a, b in zip(sums["d", k - 1], arrived_up)]
            sums["u", k - 1] = [added(a, b) for a, b in zip(sums["u", k - 1], arrived_down)]
    sections = lax.axis_size("section")
    turn = [(source, (source + 1) % sections) for source in range(sections)]
    final = [added(*terms) for terms in zip(pieces, sums["d", 0], arrived_up, arrived_down)]
    advanced = jnp.concatenate([lax.ppermute(v, "section", turn) for v in final], axis=0)[None]

    row = jnp.arange(rows, dtype=jnp.int32)
    picked = None
    for slot in order:
        one_hot = (needles[0][:, None] == (row + blocks[line[slot]] * rows)[None, :]).astype(jnp.bfloat16)
        term = jnp.dot(one_hot, gated[slot], preferred_element_type=jnp.float32)
        picked = term if picked is None else picked + term
    return (advanced, picked.astype(jnp.bfloat16)[None])


def solution(mesh):
    return jax.shard_map(
        on_device,
        mesh=mesh,
        in_specs=(
            P("section", ("groups", "ctx"), "mp"),
            P("section", "mp"),
            P("section", "mp", None, "ctx"),
            P("section", "ctx", None),
            P("section", "ctx", "mp"),
            P(("groups", "section")),
            P("section", "groups"),
        ),
        out_specs=(P("section", ("groups", "ctx"), "mp"), P("section", "groups", "ctx")),
        check_vma=False,
    )
```

```python
import functools

import jax
import jax.numpy as jnp
import ml_dtypes
import numpy as np
from jax import lax
from jax.experimental import pallas as pl
from jax.experimental.pallas import tpu as pltpu
from jax.sharding import PartitionSpec as P


norm_eps = 1e-06
lanes = 128
halves = 2
vmem_limit = 40 * 1024 * 1024


def tile_of(extent, most):
    tile = min(extent, most)
    while extent % tile:
        tile //= 2
    return tile


def smem():
    return pl.BlockSpec(memory_space=pltpu.SMEM)


def params():
    return pltpu.CompilerParams(vmem_limit_bytes=vmem_limit)


def project_kernel(merged, parts, line, first, final, table_ref, gain_ref, *refs):
    step = pl.program_id(0)
    x_refs = refs[:parts]
    carry_ref = None if first else refs[parts]
    w_ref, _, out_ref, scaled, stat = refs[parts + (0 if first else 1) :]
    tile = out_ref.shape[1]
    busy = table_ref[line, 4] > 0
    last = step == pl.num_programs(0) - 1

    @pl.when(busy & (step == 0))
    def _():
        streams = parts // 2 if merged else parts
        chunk = x_refs[0].shape[0]
        for index in range(streams):
            x = x_refs[index][...].astype(jnp.float32)
            if merged:
                x = x + x_refs[streams + index][...].astype(jnp.float32)
            place = slice(index * chunk, (index + 1) * chunk)
            scaled[place, :] = (x * gain_ref[...]).astype(jnp.bfloat16)
            stat[place, :] = jnp.broadcast_to(jnp.sum(x * x, axis=1, keepdims=True), (chunk, lanes))

    @pl.when(busy & jnp.logical_not(last))
    def _():
        total = jnp.dot(scaled[...], w_ref[0], preferred_element_type=jnp.float32)
        if not first:
            total = total + carry_ref[...]
        out_ref[...] = total.astype(out_ref.dtype)

    @pl.when(busy & last)
    def _():
        squares = stat[...]
        if not first:
            squares = squares + carry_ref[:, :lanes]
        if final:
            high = squares.astype(jnp.bfloat16).astype(jnp.float32)
            column = lax.broadcasted_iota(jnp.int32, squares.shape, 1)
            squares = jnp.where(column == 0, high, jnp.where(column == 1, squares - high, 0.0))
        out_ref[:, :lanes] = squares.astype(out_ref.dtype)
        if tile > lanes:
            out_ref[:, lanes:] = jnp.zeros((out_ref.shape[0], tile - lanes), out_ref.dtype)

    @pl.when(jnp.logical_not(busy))
    def _():
        out_ref[...] = jnp.zeros_like(out_ref)


def project(pieces, merged, table, line, gain, w, part, carry, final, after):
    streams, _, channels = w.shape
    rows_each, depth = pieces[0].shape
    rows = rows_each * (len(pieces) // 2 if merged else len(pieces))
    tile = tile_of(channels, 1024)
    per = channels // tile
    steps = streams * per
    first = carry is None

    def weights(i):
        j = jnp.minimum(i, steps - 1)
        return (j // per, part, j % per)

    column = pl.BlockSpec((rows, tile), lambda i: (0, i))
    return pl.pallas_call(
        functools.partial(project_kernel, merged, len(pieces), line, first, final),
        grid=(steps + 1,),
        in_specs=[smem(), pl.BlockSpec((1, depth), lambda i: (0, part))]
        + [pl.BlockSpec((rows_each, depth), lambda i: (0, 0))] * len(pieces)
        + ([] if first else [column])
        + [pl.BlockSpec((1, depth, tile), weights), pl.BlockSpec(memory_space=pl.ANY)],
        out_specs=column,
        out_shape=jax.ShapeDtypeStruct(
            (rows, streams * channels + lanes), jnp.bfloat16 if final else jnp.float32
        ),
        scratch_shapes=[pltpu.VMEM((rows, depth), jnp.bfloat16), pltpu.VMEM((rows, lanes), jnp.float32)],
        compiler_params=params(),
        cost_estimate=pl.CostEstimate(
            flops=2 * rows * depth * streams * channels,
            bytes_accessed=2 * streams * depth * channels,
            transcendentals=0,
        ),
        name="project",
    )(table, gain, *pieces, *(() if first else (carry,)), w, after)


def wave_tables(rows):
    window = 2 * rows
    angle = np.pi / window * (2 * np.arange(rows)[:, None] + 1) * np.arange(window)[None, :]
    forward = np.concatenate([np.cos(angle), np.sin(angle)], axis=0)
    inverse = forward[:, rows:].T * (2.0 / window)

    def pair(matrix):
        exact = jnp.asarray(matrix, jnp.float32)
        high = jnp.asarray(np.asarray(matrix, ml_dtypes.bfloat16))
        low = jnp.asarray(np.asarray(matrix - np.asarray(matrix, ml_dtypes.bfloat16).astype(np.float64), ml_dtypes.bfloat16))
        return high, low

    high, low = pair(forward)
    inverse_high, inverse_low = pair(inverse)
    return jnp.concatenate([high, low], axis=0), jnp.concatenate([inverse_high, inverse_low], axis=0)


def spectrum_kernel(taps_ref, forward_ref, _, out_ref):
    taps = taps_ref.shape[1]
    both = lax.dot_general(
        forward_ref[:, :taps], taps_ref[...], (((1,), (1,)), ((), ())), preferred_element_type=jnp.float32
    )
    half = out_ref.shape[0]
    out_ref[...] = both[:half, :] + both[half:, :]


def spectrum(taps, forward, after):
    channels = taps.shape[0]
    tile = tile_of(channels, 256)
    window = forward.shape[1]
    return pl.pallas_call(
        spectrum_kernel,
        grid=(channels // tile,),
        in_specs=[
            pl.BlockSpec((tile, taps.shape[1]), lambda i: (i, 0)),
            pl.BlockSpec(forward.shape, lambda i: (0, 0)),
            pl.BlockSpec(memory_space=pl.ANY),
        ],
        out_specs=pl.BlockSpec((window, tile), lambda i: (0, i)),
        out_shape=jax.ShapeDtypeStruct((window, channels), jnp.float32),
        compiler_params=params(),
        name="spectrum",
    )(taps, forward, after)


def mix_kernel(full_width, line, table_ref, *refs):
    q0, k0, v0, s0, q1, k1, v1, s1, pk0, pv0, ps0, pk1, pv1, ps1, f_ref, forward_ref, inverse_ref, _, out_ref, window = refs
    rows = out_ref.shape[0]
    block = table_ref[line, 0]
    length = table_ref[line, 1]
    work = table_ref[line, 2] > 0

    def joined(a_ref, b_ref):
        return a_ref[...].astype(jnp.float32) + b_ref[...].astype(jnp.float32)

    def inverse_norm(a_ref, b_ref):
        mean = jnp.sum(joined(a_ref, b_ref), axis=1, keepdims=True) / full_width
        return lax.rsqrt(mean + norm_eps)

    @pl.when(work)
    def _():
        row = lax.broadcasted_iota(jnp.int32, (rows, 1), 0)
        scale = inverse_norm(s0, s1)
        live = (row + block * rows < length).astype(jnp.float32)
        here = joined(k0, k1) * scale * (joined(v0, v1) * scale) * live
        window[rows:, :] = here.astype(jnp.bfloat16)

        @pl.when(table_ref[line, 3] > 0)
        def _():
            scale = inverse_norm(ps0, ps1)
            live = (row + (block - 1) * rows < length).astype(jnp.float32)
            before = joined(pk0, pk1) * scale * (joined(pv0, pv1) * scale) * live
            window[:rows, :] = before.astype(jnp.bfloat16)

        @pl.when(table_ref[line, 3] == 0)
        def _():
            window[:rows, :] = jnp.zeros((rows, window.shape[1]), jnp.bfloat16)

        both = jnp.dot(forward_ref[...], window[...], preferred_element_type=jnp.float32)
        cosine = both[:rows, :] + both[2 * rows : 3 * rows, :]
        sine = both[rows : 2 * rows, :] + both[3 * rows :, :]
        f_cosine = f_ref[:rows, :]
        f_sine = f_ref[rows:, :]
        product = jnp.concatenate(
            [cosine * f_cosine - sine * f_sine, cosine * f_sine + sine * f_cosine], axis=0
        )
        high = product.astype(jnp.bfloat16)
        low = (product - high.astype(jnp.float32)).astype(jnp.bfloat16)
        back = jnp.dot(inverse_ref[...], high, preferred_element_type=jnp.float32)
        conv = back[:rows, :] + back[rows:, :]
        conv = conv + jnp.dot(inverse_ref[:rows, :], low, preferred_element_type=jnp.float32)
        out_ref[...] = (joined(q0, q1) * scale * conv * live).astype(jnp.bfloat16)

    @pl.when(jnp.logical_not(work))
    def _():
        out_ref[...] = jnp.zeros_like(out_ref)


def mix(table, line, here, before, rows, waves, filter_waves, full_width, after):
    own, got, at = here
    own_before, got_before, at_before = before
    forward, inverse = waves
    channels = filter_waves.shape[1]
    tile = tile_of(channels, 256)
    per = channels // tile
    streams = 3

    def spec(at, stream):
        return pl.BlockSpec((rows, tile), lambda i: (at, stream * per + i))

    def stat(at):
        return pl.BlockSpec((rows, lanes), lambda i: (at, streams * (channels // lanes)))

    whole = [pl.BlockSpec(wave.shape, lambda i: (0, 0)) for wave in waves]
    return pl.pallas_call(
        functools.partial(mix_kernel, full_width, line),
        grid=(per,),
        in_specs=[smem()]
        + [spec(at, 0), spec(at, 1), spec(at, 2), stat(at)] * 2
        + [spec(at_before, 1), spec(at_before, 2), stat(at_before)] * 2
        + [pl.BlockSpec((2 * rows, tile), lambda i: (0, i))]
        + whole
        + [pl.BlockSpec(memory_space=pl.ANY)],
        out_specs=pl.BlockSpec((rows, tile), lambda i: (0, i)),
        out_shape=jax.ShapeDtypeStruct((rows, channels), jnp.bfloat16),
        scratch_shapes=[pltpu.VMEM((2 * rows, tile), jnp.bfloat16)],
        compiler_params=params(),
        cost_estimate=pl.CostEstimate(
            flops=16 * rows * rows * channels, bytes_accessed=32 * rows * channels, transcendentals=0
        ),
        name="mix",
    )(
        table, own, own, own, own, got, got, got, got,
        own_before, own_before, own_before, got_before, got_before, got_before,
        filter_waves, forward, inverse, after,
    )


def emit_kernel(line, table_ref, gated_ref, w_ref, _, *out_refs):
    work = table_ref[line, 2] > 0
    chunk = out_refs[0].shape[0]

    @pl.when(work)
    def _():
        product = jnp.dot(gated_ref[...], w_ref[...], preferred_element_type=jnp.float32).astype(jnp.bfloat16)
        for index, out_ref in enumerate(out_refs):
            out_ref[...] = product[index * chunk : (index + 1) * chunk, :]

    @pl.when(jnp.logical_not(work))
    def _():
        for out_ref in out_refs:
            out_ref[...] = jnp.zeros_like(out_ref)


def emit(table, line, gated, w, after):
    rows, channels = gated.shape
    width = w.shape[1]
    tile = tile_of(width, 1024)
    chunk = rows // halves
    return pl.pallas_call(
        functools.partial(emit_kernel, line),
        grid=(width // tile,),
        in_specs=[
            smem(),
            pl.BlockSpec((rows, channels), lambda i: (0, 0)),
            pl.BlockSpec((channels, tile), lambda i: (0, i)),
            pl.BlockSpec(memory_space=pl.ANY),
        ],
        out_specs=[pl.BlockSpec((chunk, tile), lambda i: (0, i))] * halves,
        out_shape=[jax.ShapeDtypeStruct((chunk, width), jnp.bfloat16)] * halves,
        compiler_params=params(),
        cost_estimate=pl.CostEstimate(
            flops=2 * rows * channels * width, bytes_accessed=2 * channels * width, transcendentals=0
        ),
        name="emit",
    )(table, gated, w, after)


def added(*terms):
    total = terms[0].astype(jnp.float32)
    for term in terms[1:]:
        total = total + term.astype(jnp.float32)
    return total.astype(jnp.bfloat16)


def layer(spans, norm_gain, w_in, filters, w_out, prompt_len, needles):
    count = lax.axis_size("ctx")
    place = lax.axis_index("ctx")
    x_local = spans[0]
    rows, half_width = x_local.shape
    chunk = rows // halves
    full_width = half_width * lax.axis_size("mp")
    weights = jnp.swapaxes(w_in[0], 0, 1)
    gain = norm_gain
    up = [(source, source + 1) for source in range(count - 1)]
    down = [(source + 1, source) for source in range(count - 1)]
    partner = [(0, 1), (1, 0)] if lax.axis_size("mp") == 2 else None

    far = count - 1
    order = [("d", 0)] + [(kind, k) for k in range(1, far) for kind in "du"] + [("m", far)]
    line = {slot: index for index, slot in enumerate(order)}
    z = place.astype(jnp.int32)
    reach = jnp.array([k for _, k in order], jnp.int32)
    kinds = jnp.array(["dum".index(kind) for kind, _ in order], jnp.int32)
    downward = (kinds == 0) | ((kinds == 2) & (z == 0))
    blocks = jnp.where(downward, z + reach, z - reach)
    work = (blocks >= 0) & (blocks < count)
    busy = (z - reach >= 0) | (z + reach < count)
    table = jnp.stack(
        [blocks, jnp.broadcast_to(prompt_len[0], blocks.shape), work, (blocks >= 1) & work, busy], axis=1
    ).astype(jnp.int32)

    part = half_width // halves
    waves = wave_tables(rows)
    pieces = [x_local[:, i * part : (i + 1) * part] for i in range(halves)]
    gathered = {("d", 0): pieces, ("u", 0): pieces}
    for k in range(1, count):
        gathered["u", k] = []
        gathered["d", k] = []
        for i in range(halves):
            value = lax.ppermute(gathered["u", k - 1][i], "ctx", [(a, b) for a, b in up if a >= k - 1])
            gathered["u", k].append(value)
            value = lax.ppermute(gathered["d", k - 1][i], "ctx", [(a, b) for a, b in down if a <= count - k])
            gathered["d", k].append(value)

    after = x_local
    held = {}

    def offer(k, own):
        merged = 2 * k >= count
        got = lax.ppermute(own, "mp", partner)
        held["u", k] = (own, got, 0)
        held["d", k] = (own, got, 0 if merged or k == 0 else 1)

    gated = {}
    sums = {}

    def blend(kind, k, after):
        before = ("u", k + 1) if kind == "u" or k == 0 else ("d", k - 1)
        gated[kind, k] = mix(
            table, line[kind, k], held["d" if kind == "m" else kind, k], held[before],
            rows, waves, filter_waves, full_width, after,
        )
        sums[kind, k] = emit(table, line[kind, k], gated[kind, k], w_out[0], gated[kind, k])
        return sums[kind, k][0]

    after = project([x_local], False, table, 0, gain, weights, 0, None, True, after)
    offer(0, after)
    filter_waves = spectrum(filters[0], waves[0], after)
    after = filter_waves
    for k in range(1, count):
        slot = ("d", k) if k < far else ("m", far)
        carry = None
        for i in range(halves):
            after = project(
                [gathered["u", k][i], gathered["d", k][i]],
                2 * k >= count, table, line[slot], gain, weights, i, carry, i == halves - 1, after,
            )
            carry = after
        offer(k, after)
    after = blend("m", far, after)
    for k in range(far - 1, 0, -1):
        after = blend("u", k, after)
        after = blend("d", k, after)
    after = blend("d", 0, after)

    def reduce_step(values, pairs):
        moved = []
        for value in values:
            moved.append(lax.ppermute(value, "ctx", pairs))
        return moved

    terms = [sums["d", 0]]
    for k in range(far, 0, -1):
        to_up = [(a, b) for a, b in up if a + k <= far]
        to_down = [(a, b) for a, b in down if a >= k]
        if k == far and far != 2:
            arrived = [reduce_step(sums["m", far], to_up + to_down)] * 2
        else:
            from_up, from_down = ("m", "m") if k == far else ("d", "u")
            arrived = [reduce_step(sums[from_up, k], to_up), reduce_step(sums[from_down, k], to_down)]
        if k > 1:
            for kind, moved in zip("du", arrived):
                sums[kind, k - 1] = [added(a, b) for a, b in zip(sums[kind, k - 1], moved)]
        else:
            terms += arrived if far > 1 else arrived[:1]
    pieces = [x_local[i * chunk : (i + 1) * chunk] for i in range(halves)]
    sections = lax.axis_size("section")
    turn = [(source, (source + 1) % sections) for source in range(sections)]
    final = [added(*parts) for parts in zip(pieces, *terms)]
    advanced = jnp.concatenate([lax.ppermute(v, "section", turn) for v in final], axis=0)[None]

    row = jnp.arange(rows, dtype=jnp.int32)
    picked = None
    for slot in order:
        one_hot = (needles[0][:, None] == (row + blocks[line[slot]] * rows)[None, :]).astype(jnp.bfloat16)
        term = jnp.dot(one_hot, gated[slot], preferred_element_type=jnp.float32)
        picked = term if picked is None else picked + term
    return (advanced, picked.astype(jnp.bfloat16)[None])


def solution(mesh):
    return jax.shard_map(
        layer,
        mesh=mesh,
        in_specs=(
            P("section", ("groups", "ctx"), "mp"),
            P("section", "mp"),
            P("section", "mp", None, "ctx"),
            P("section", "ctx", None),
            P("section", "ctx", "mp"),
            P(("groups", "section")),
            P("section", "groups"),
        ),
        out_specs=(P("section", ("groups", "ctx"), "mp"), P("section", "groups", "ctx")),
        check_vma=False,
    )
```

```python
import functools

import jax
import jax.numpy as jnp
import ml_dtypes
import numpy as np
from jax import lax
from jax.experimental import pallas as pl
from jax.experimental.pallas import tpu as pltpu
from jax.sharding import PartitionSpec as P


norm_eps = 1e-06
lanes = 128
halves = 2
vmem_limit = 40 * 1024 * 1024


def tile_of(extent, most):
    tile = min(extent, most)
    while extent % tile:
        tile //= 2
    return tile


def smem():
    return pl.BlockSpec(memory_space=pltpu.SMEM)


def params():
    return pltpu.CompilerParams(vmem_limit_bytes=vmem_limit)


def project_kernel(layout, first, final, *refs):
    refs = refs[1:] if final else refs
    gain_ref, *refs = refs
    x_refs = refs[: sum(layout)]
    refs = refs[sum(layout) :]
    carry_refs = () if first else refs[:2]
    refs = refs if first else refs[2:]
    w_ref, _, out_ref, *more, scaled, stat = refs
    step = pl.program_id(0)
    last = step == pl.num_programs(0) - 1

    @pl.when(step == 0)
    def _():
        chunk = x_refs[0].shape[0]
        source = 0
        for index, inputs in enumerate(layout):
            x = x_refs[source][...].astype(jnp.float32)
            for other in range(1, inputs):
                x = x + x_refs[source + other][...].astype(jnp.float32)
            source += inputs
            place = slice(index * chunk, (index + 1) * chunk)
            scaled[place, :] = (x * gain_ref[...]).astype(jnp.bfloat16)
            squares = jnp.broadcast_to(jnp.sum(x * x, axis=1, keepdims=True), (chunk, lanes))
            stat[place, :] = squares if first else squares + carry_refs[1][place, :]

    def product():
        total = jnp.dot(scaled[...], w_ref[0], preferred_element_type=jnp.float32)
        if not first:
            total = total + carry_refs[0][...]
        out_ref[...] = total.astype(out_ref.dtype)

    if not final:
        product()
        more[0][...] = stat[...]
        return

    pl.when(jnp.logical_not(last))(product)

    @pl.when(last)
    def _():
        squares = stat[...]
        high = squares.astype(jnp.bfloat16).astype(jnp.float32)
        column = lax.broadcasted_iota(jnp.int32, squares.shape, 1)
        squares = jnp.where(column == 0, high, jnp.where(column == 1, squares - high, 0.0))
        out_ref[:, :lanes] = squares.astype(out_ref.dtype)
        if out_ref.shape[1] > lanes:
            out_ref[:, lanes:] = jnp.zeros((out_ref.shape[0], out_ref.shape[1] - lanes), out_ref.dtype)


def project(pieces, layout, gain, w, part, carry, side, sides, after):
    streams, _, channels = w.shape
    chunk, depth = pieces[0].shape
    rows = chunk * len(layout)
    final = side is not None
    first = carry is None
    tile = channels // 2
    steps = streams if final else 2 * streams

    def channel(i, held):
        return (jnp.minimum(i, steps - 1) * 2 + held[side]) if final else i

    def at(index):
        return lambda i, *held: index(i, held[0] if final else None)

    column = pl.BlockSpec((rows, tile), at(lambda i, held: (0, channel(i, held))))
    whole_stat = pl.BlockSpec((rows, lanes), at(lambda i, held: (0, 0)))
    out_specs = [pl.BlockSpec((rows, tile), at(lambda i, held: (0, i)))]
    out_shape = [jax.ShapeDtypeStruct((rows, streams * tile + lanes), jnp.bfloat16)]
    if not final:
        out_specs.append(whole_stat)
        out_shape = [
            jax.ShapeDtypeStruct((rows, streams * channels), jnp.float32),
            jax.ShapeDtypeStruct((rows, lanes), jnp.float32),
        ]
    result = pl.pallas_call(
        functools.partial(project_kernel, layout, first, final),
        grid_spec=pltpu.PrefetchScalarGridSpec(
            num_scalar_prefetch=1 if final else 0,
            grid=(steps + 1 if final else steps,),
            in_specs=[pl.BlockSpec((1, depth), at(lambda i, held: (0, part)))]
            + [pl.BlockSpec((chunk, depth), at(lambda i, held: (0, 0)))] * len(pieces)
            + ([] if first else [column, whole_stat])
            + [
                pl.BlockSpec(
                    (1, depth, tile),
                    at(lambda i, held: (channel(i, held) // 2, part, channel(i, held) % 2)),
                ),
                pl.BlockSpec(memory_space=pl.ANY),
            ],
            out_specs=out_specs,
            scratch_shapes=[pltpu.VMEM((rows, depth), jnp.bfloat16), pltpu.VMEM((rows, lanes), jnp.float32)],
        ),
        out_shape=out_shape,
        compiler_params=params(),
        cost_estimate=pl.CostEstimate(
            flops=2 * rows * depth * steps * tile, bytes_accessed=2 * depth * steps * tile, transcendentals=0
        ),
        name="project",
    )(*((sides,) if final else ()), gain, *pieces, *(() if first else carry), w, after)
    return result[0] if final else tuple(result)


def wave_tables(rows):
    window = 2 * rows
    angle = np.pi / window * (2 * np.arange(rows)[:, None] + 1) * np.arange(window)[None, :]
    forward = np.concatenate([np.cos(angle), np.sin(angle)], axis=0)
    inverse = forward[:, rows:].T * (2.0 / window)

    def pair(matrix):
        exact = jnp.asarray(matrix, jnp.float32)
        high = jnp.asarray(np.asarray(matrix, ml_dtypes.bfloat16))
        low = jnp.asarray(np.asarray(matrix - np.asarray(matrix, ml_dtypes.bfloat16).astype(np.float64), ml_dtypes.bfloat16))
        return high, low

    high, low = pair(forward)
    inverse_high, inverse_low = pair(inverse)
    return jnp.concatenate([high, low], axis=0), jnp.concatenate([inverse_high, inverse_low], axis=0)


def spectrum_kernel(taps_ref, forward_ref, _, out_ref):
    taps = taps_ref.shape[1]
    both = lax.dot_general(
        forward_ref[:, :taps], taps_ref[...], (((1,), (1,)), ((), ())), preferred_element_type=jnp.float32
    )
    half = out_ref.shape[0]
    out_ref[...] = both[:half, :] + both[half:, :]


def spectrum(taps, forward, after):
    channels = taps.shape[0]
    tile = tile_of(channels, 256)
    window = forward.shape[1]
    return pl.pallas_call(
        spectrum_kernel,
        grid=(channels // tile,),
        in_specs=[
            pl.BlockSpec((tile, taps.shape[1]), lambda i: (i, 0)),
            pl.BlockSpec(forward.shape, lambda i: (0, 0)),
            pl.BlockSpec(memory_space=pl.ANY),
        ],
        out_specs=pl.BlockSpec((window, tile), lambda i: (0, i)),
        out_shape=jax.ShapeDtypeStruct((window, channels), jnp.float32),
        compiler_params=params(),
        name="spectrum",
    )(taps, forward, after)


def mix_kernel(full_width, line, sides_ref, table_ref, *refs):
    q0, k0, v0, s0, q1, k1, v1, s1, pk0, pv0, ps0, pk1, pv1, ps1, f_ref, forward_ref, inverse_ref, _, out_ref, window = refs
    rows = out_ref.shape[0]
    block = table_ref[line, 0]
    length = table_ref[line, 1]
    work = table_ref[line, 2] > 0

    def joined(a_ref, b_ref):
        return a_ref[...].astype(jnp.float32) + b_ref[...].astype(jnp.float32)

    def inverse_norm(a_ref, b_ref):
        mean = jnp.sum(joined(a_ref, b_ref), axis=1, keepdims=True) / full_width
        return lax.rsqrt(mean + norm_eps)

    @pl.when(work)
    def _():
        row = lax.broadcasted_iota(jnp.int32, (rows, 1), 0)
        scale = inverse_norm(s0, s1)
        live = (row + block * rows < length).astype(jnp.float32)
        here = joined(k0, k1) * scale * (joined(v0, v1) * scale) * live
        window[rows:, :] = here.astype(jnp.bfloat16)

        @pl.when(table_ref[line, 3] > 0)
        def _():
            scale = inverse_norm(ps0, ps1)
            live = (row + (block - 1) * rows < length).astype(jnp.float32)
            before = joined(pk0, pk1) * scale * (joined(pv0, pv1) * scale) * live
            window[:rows, :] = before.astype(jnp.bfloat16)

        @pl.when(table_ref[line, 3] == 0)
        def _():
            window[:rows, :] = jnp.zeros((rows, window.shape[1]), jnp.bfloat16)

        both = jnp.dot(forward_ref[...], window[...], preferred_element_type=jnp.float32)
        cosine = both[:rows, :] + both[2 * rows : 3 * rows, :]
        sine = both[rows : 2 * rows, :] + both[3 * rows :, :]
        f_cosine = f_ref[:rows, :]
        f_sine = f_ref[rows:, :]
        product = jnp.concatenate(
            [cosine * f_cosine - sine * f_sine, cosine * f_sine + sine * f_cosine], axis=0
        )
        high = product.astype(jnp.bfloat16)
        low = (product - high.astype(jnp.float32)).astype(jnp.bfloat16)
        back = jnp.dot(inverse_ref[...], high, preferred_element_type=jnp.float32)
        conv = back[:rows, :] + back[rows:, :]
        conv = conv + jnp.dot(inverse_ref[:rows, :], low, preferred_element_type=jnp.float32)
        out_ref[...] = (joined(q0, q1) * scale * conv * live).astype(jnp.bfloat16)

    @pl.when(jnp.logical_not(work))
    def _():
        out_ref[...] = jnp.zeros_like(out_ref)


def mix(table, line, here, before, rows, waves, filter_waves, full_width, sides, after):
    own, got, at = here
    own_before, got_before, at_before = before
    channels = filter_waves.shape[1] // 2
    tile = tile_of(channels, 256)
    per = channels // tile
    streams = 3

    def spec(at, stream):
        return pl.BlockSpec((rows, tile), lambda i, held: (at, stream * per + i))

    def stat(at):
        return pl.BlockSpec((rows, lanes), lambda i, held: (at, streams * (channels // lanes)))

    whole = [pl.BlockSpec(wave.shape, lambda i, held: (0, 0)) for wave in waves]
    return pl.pallas_call(
        functools.partial(mix_kernel, full_width, line),
        grid_spec=pltpu.PrefetchScalarGridSpec(
            num_scalar_prefetch=1,
            grid=(per,),
            in_specs=[smem()]
            + [spec(at, 0), spec(at, 1), spec(at, 2), stat(at)] * 2
            + [spec(at_before, 1), spec(at_before, 2), stat(at_before)] * 2
            + [pl.BlockSpec((2 * rows, tile), lambda i, held: (0, held[0] * per + i))]
            + whole
            + [pl.BlockSpec(memory_space=pl.ANY)],
            out_specs=pl.BlockSpec((rows, tile), lambda i, held: (0, i)),
            scratch_shapes=[pltpu.VMEM((2 * rows, tile), jnp.bfloat16)],
        ),
        out_shape=jax.ShapeDtypeStruct((rows, channels), jnp.bfloat16),
        compiler_params=params(),
        cost_estimate=pl.CostEstimate(
            flops=16 * rows * rows * channels, bytes_accessed=32 * rows * channels, transcendentals=0
        ),
        name="mix",
    )(
        sides, table, own, own, own, own, got, got, got, got,
        own_before, own_before, own_before, got_before, got_before, got_before,
        filter_waves, *waves, after,
    )


def emit_kernel(line, sides_ref, table_ref, mine_ref, theirs_ref, w_mine_ref, w_theirs_ref, _, *out_refs):
    work = table_ref[line, 2] > 0
    chunk = out_refs[0].shape[0]

    @pl.when(work)
    def _():
        product = jnp.dot(mine_ref[...], w_mine_ref[...], preferred_element_type=jnp.float32)
        product = product + jnp.dot(theirs_ref[...], w_theirs_ref[...], preferred_element_type=jnp.float32)
        product = product.astype(jnp.bfloat16)
        for index, out_ref in enumerate(out_refs):
            out_ref[...] = product[index * chunk : (index + 1) * chunk, :]

    @pl.when(jnp.logical_not(work))
    def _():
        for out_ref in out_refs:
            out_ref[...] = jnp.zeros_like(out_ref)


def emit(table, line, mine, theirs, w, sides, after):
    rows, half = mine.shape
    width = w.shape[1]
    tile = tile_of(width, 1024)
    chunk = rows // halves
    whole = pl.BlockSpec((rows, half), lambda i, held: (0, 0))
    return pl.pallas_call(
        functools.partial(emit_kernel, line),
        grid_spec=pltpu.PrefetchScalarGridSpec(
            num_scalar_prefetch=1,
            grid=(width // tile,),
            in_specs=[
                smem(),
                whole,
                whole,
                pl.BlockSpec((half, tile), lambda i, held: (held[0], i)),
                pl.BlockSpec((half, tile), lambda i, held: (held[1], i)),
                pl.BlockSpec(memory_space=pl.ANY),
            ],
            out_specs=[pl.BlockSpec((chunk, tile), lambda i, held: (0, i))] * halves,
        ),
        out_shape=[jax.ShapeDtypeStruct((chunk, width), jnp.bfloat16)] * halves,
        compiler_params=params(),
        cost_estimate=pl.CostEstimate(
            flops=4 * rows * half * width, bytes_accessed=4 * half * width, transcendentals=0
        ),
        name="emit",
    )(sides, table, mine, theirs, w, w, after)


def finish_kernel(*refs):
    total = refs[0][...].astype(jnp.float32)
    for ref in refs[1:-1]:
        total = total + ref[...].astype(jnp.float32)
    refs[-1][...] = total.astype(jnp.bfloat16)


def finish(x, index, terms):
    chunk, width = terms[0].shape
    tile = tile_of(width, 1024)
    return pl.pallas_call(
        finish_kernel,
        grid=(width // tile,),
        in_specs=[pl.BlockSpec((chunk, tile), lambda i: (index, i))]
        + [pl.BlockSpec((chunk, tile), lambda i: (0, i))] * len(terms),
        out_specs=pl.BlockSpec((chunk, tile), lambda i: (0, i)),
        out_shape=jax.ShapeDtypeStruct((chunk, width), jnp.bfloat16),
        compiler_params=params(),
        cost_estimate=pl.CostEstimate(
            flops=chunk * width * len(terms), bytes_accessed=2 * chunk * width * (len(terms) + 2), transcendentals=0
        ),
        name="finish",
    )(x, *terms)


def added(*terms):
    total = terms[0].astype(jnp.float32)
    for term in terms[1:]:
        total = total + term.astype(jnp.float32)
    return total.astype(jnp.bfloat16)


def layer(spans, norm_gain, w_in, filters, w_out, prompt_len, needles):
    count = lax.axis_size("ctx")
    place = lax.axis_index("ctx")
    x_local = spans[0]
    rows, half_width = x_local.shape
    full_width = half_width * lax.axis_size("mp")
    weights = jnp.swapaxes(w_in[0], 0, 1)
    gain = norm_gain
    up = [(source, source + 1) for source in range(count - 1)]
    down = [(source + 1, source) for source in range(count - 1)]
    partner = [(0, 1), (1, 0)] if lax.axis_size("mp") == 2 else None

    far = count - 1
    order = [("d", 0)] + [(kind, k) for k in range(1, far) for kind in "du"] + [("m", far)]
    line = {slot: index for index, slot in enumerate(order)}
    z = place.astype(jnp.int32)
    reach = jnp.array([k for _, k in order], jnp.int32)
    kinds = jnp.array(["dum".index(kind) for kind, _ in order], jnp.int32)
    downward = (kinds == 0) | ((kinds == 2) & (z == 0))
    blocks = jnp.where(downward, z + reach, z - reach)
    work = (blocks >= 0) & (blocks < count)
    busy = (z - reach >= 0) | (z + reach < count)
    table = jnp.stack(
        [blocks, jnp.broadcast_to(prompt_len[0], blocks.shape), work, (blocks >= 1) & work, busy], axis=1
    ).astype(jnp.int32)

    part = half_width // halves
    waves = wave_tables(rows)
    pieces = [x_local[:, i * part : (i + 1) * part] for i in range(halves)]
    gathered = {("d", 0): pieces, ("u", 0): pieces}
    for k in range(1, count):
        gathered["u", k] = []
        gathered["d", k] = []
        for i in range(halves):
            value = lax.ppermute(gathered["u", k - 1][i], "ctx", [(a, b) for a, b in up if a >= k - 1])
            gathered["u", k].append(value)
            value = lax.ppermute(gathered["d", k - 1][i], "ctx", [(a, b) for a, b in down if a <= count - k])
            gathered["d", k].append(value)

    core = lax.axis_index("mp").astype(jnp.int32)
    sides = jnp.stack([core, 1 - core])
    held = {}
    gated = {}
    sums = {}

    def combine(kind, k, after):
        before = ("u", k + 1) if kind == "u" or k == 0 else ("d", k - 1)
        mine = mix(
            table, line[kind, k], held["d" if kind == "m" else kind, k], held[before],
            rows, waves, filter_waves, full_width, sides, after,
        )
        gated[kind, k] = (mine, lax.ppermute(mine, "mp", partner))
        return mine

    def spread(kind, k, after):
        sums[kind, k] = emit(table, line[kind, k], *gated[kind, k], w_out[0], sides, after)
        return sums[kind, k][0]

    filter_waves = spectrum(filters[0], waves[0], x_local)
    after = filter_waves
    for group in groups_of(count):
        layout = []
        inputs = [[] for _ in range(halves)]
        for k in group:
            merged = 2 * k >= count
            for kind in ("d",) if k == 0 else ("ud",) if merged else ("u", "d"):
                for way in kind:
                    held[way, k] = len(layout)
                    for i in range(halves):
                        inputs[i].append(gathered[way, k][i])
                layout.append(len(kind))
        carry = None
        for i in range(halves - 1):
            carry = project(inputs[i], layout, gain, weights, i, carry, None, sides, after)
            after = carry[1]
        theirs = project(inputs[-1], layout, gain, weights, halves - 1, carry, 1, sides, after)
        got = lax.ppermute(theirs, "mp", partner)
        mine = project(inputs[-1], layout, gain, weights, halves - 1, carry, 0, sides, theirs)
        after = mine
        for k in group:
            for way in "d" if k == 0 else "ud":
                held[way, k] = (mine, got, held[way, k])
        for kind, k in early_slots(count) if group[0] == 0 else ():
            after = combine(kind, k, after)
        for kind, k in early_slots(count) if group[0] == 0 else ():
            after = spread(kind, k, after)
    rest = [slot for slot in [("m", far)] + [(kind, k) for k in range(far - 1, 0, -1) for kind in "ud"] + [("d", 0)]]
    rest = [slot for slot in rest if slot not in sums]
    after = combine(*rest[0], after)
    for index, slot in enumerate(rest):
        if index + 1 < len(rest):
            after = combine(*rest[index + 1], after)
        after = spread(*slot, after)

    def reduce_step(values, pairs):
        moved = []
        for value in values:
            moved.append(lax.ppermute(value, "ctx", pairs))
        return moved

    terms = [sums["d", 0]]
    for k in range(far, 0, -1):
        to_up = [(a, b) for a, b in up if a + k <= far]
        to_down = [(a, b) for a, b in down if a >= k]
        if k == far and far != 2:
            arrived = [reduce_step(sums["m", far], to_up + to_down)] * 2
        else:
            from_up, from_down = ("m", "m") if k == far else ("d", "u")
            arrived = [reduce_step(sums[from_up, k], to_up), reduce_step(sums[from_down, k], to_down)]
        if k > 1:
            for kind, moved in zip("du", arrived):
                sums[kind, k - 1] = [added(a, b) for a, b in zip(sums[kind, k - 1], moved)]
        else:
            terms += arrived if far > 1 else arrived[:1]
    sections = lax.axis_size("section")
    turn = [(source, (source + 1) % sections) for source in range(sections)]
    advanced = []
    for i in range(halves):
        final = finish(x_local, i, [term[i] for term in terms])
        advanced.append(lax.ppermute(final, "section", turn))
    advanced = jnp.concatenate(advanced, axis=0)[None]

    row = jnp.arange(rows, dtype=jnp.int32)
    picked = [0.0, 0.0]
    for slot in order:
        one_hot = (needles[0][:, None] == (row + blocks[line[slot]] * rows)[None, :]).astype(jnp.bfloat16)
        for index, part in enumerate(gated[slot]):
            picked[index] += jnp.dot(one_hot, part, preferred_element_type=jnp.float32)
    mine, theirs = [value.astype(jnp.bfloat16) for value in picked]
    lower = jnp.where(core == 0, mine, theirs)
    upper = jnp.where(core == 0, theirs, mine)
    return (advanced, jnp.concatenate([lower, upper], axis=1)[None])


def groups_of(count):
    return [list(range(k, min(k + 2, count))) for k in range(0, count, 2)]


def early_slots(count):
    return [("d", 0), ("d", 1)] if count > 2 else []


def solution(mesh):
    return jax.shard_map(
        layer,
        mesh=mesh,
        in_specs=(
            P("section", ("groups", "ctx"), "mp"),
            P("section", "mp"),
            P("section", "mp", None, "ctx"),
            P("section", "ctx", None),
            P("section", "ctx", "mp"),
            P(("groups", "section")),
            P("section", "groups"),
        ),
        out_specs=(P("section", ("groups", "ctx"), "mp"), P("section", "groups", "ctx")),
        check_vma=False,
    )
```

```python
import functools

import jax
import jax.numpy as jnp
import ml_dtypes
import numpy as np
from jax import lax
from jax.experimental import pallas as pl
from jax.experimental.pallas import tpu as pltpu
from jax.sharding import PartitionSpec as P


norm_eps = 1e-06
lanes = 128
halves = 2
vmem_limit = 60 * 1024 * 1024


def tile_of(extent, most):
    tile = min(extent, most)
    while extent % tile:
        tile //= 2
    return tile


def block_of(slot, z):
    kind, k = slot[:2]
    below = z - k
    return z + k if kind == "d" else jnp.where(z == 0, k, below) if kind == "m" else below


def params():
    return pltpu.CompilerParams(vmem_limit_bytes=vmem_limit)


def prepare_kernel(x_ref, gain_ref, *refs):
    part = refs[0].shape[1]
    total = jnp.zeros((x_ref.shape[0], 1), jnp.float32)
    for index, out_ref in enumerate(refs[:-1]):
        place = slice(index * part, (index + 1) * part)
        x = x_ref[:, place].astype(jnp.float32)
        out_ref[...] = (x * gain_ref[:, place]).astype(jnp.bfloat16)
        total = total + jnp.sum(x * x, axis=1, keepdims=True)
    refs[-1][...] = jnp.broadcast_to(total, refs[-1].shape)


def prepare(x, gain):
    rows, width = x.shape
    return pl.pallas_call(
        prepare_kernel,
        out_shape=[jax.ShapeDtypeStruct((rows, width // halves), jnp.bfloat16)] * halves
        + [jax.ShapeDtypeStruct((rows, lanes), jnp.float32)],
        compiler_params=params(),
        name="prepare",
    )(x, gain)


def project_kernel(layout, parts, first, *refs):
    x_refs = refs[1 : 1 + sum(layout) * parts]
    refs = refs[1 + sum(layout) * parts :]
    carry_ref = None if first else refs[0]
    w_ref, _, out_ref, joined = refs if first else refs[1:]

    @pl.when(pl.program_id(0) == 0)
    def _():
        chunk, depth = x_refs[0].shape
        source = 0
        for part in range(parts):
            for index, inputs in enumerate(layout):
                x = x_refs[source][...]
                for other in range(1, inputs):
                    x = x + x_refs[source + other][...]
                source += inputs
                joined[index * chunk : (index + 1) * chunk, part * depth : (part + 1) * depth] = x

    total = jnp.dot(joined[...], w_ref[0], preferred_element_type=jnp.float32)
    if not first:
        total = total + carry_ref[...]
    out_ref[...] = total.astype(out_ref.dtype)


def project(pieces, layout, w, part, carry, side, info, after):
    streams, _, channels = w.shape
    chunk, depth = pieces[0][0].shape
    rows = chunk * len(layout)
    deep = depth * len(pieces)
    final = side is not None
    first = carry is None
    tile = channels // 2
    steps = streams if final else 2 * streams

    def channel(i, held):
        return i * 2 + held[side] if final else i

    column = pl.BlockSpec((rows, tile), lambda i, held: (0, channel(i, held)))
    flat = [piece for group in pieces for piece in group]
    return pl.pallas_call(
        functools.partial(project_kernel, layout, len(pieces), first),
        grid_spec=pltpu.PrefetchScalarGridSpec(
            num_scalar_prefetch=1,
            grid=(steps,),
            in_specs=[pl.BlockSpec((chunk, depth), lambda i, held: (0, 0))] * len(flat)
            + ([] if first else [column])
            + [
                pl.BlockSpec(
                    (1, deep, tile), lambda i, held: (channel(i, held) // 2, part, channel(i, held) % 2)
                ),
                pl.BlockSpec(memory_space=pl.ANY),
            ],
            out_specs=pl.BlockSpec((rows, tile), lambda i, held: (0, i)),
            scratch_shapes=[pltpu.VMEM((rows, deep), jnp.bfloat16)],
        ),
        out_shape=jax.ShapeDtypeStruct((rows, steps * tile), jnp.bfloat16 if final else jnp.float32),
        compiler_params=params(),
        cost_estimate=pl.CostEstimate(
            flops=2 * rows * deep * steps * tile, bytes_accessed=2 * deep * steps * tile, transcendentals=0
        ),
        name="project",
    )(info, *flat, *(() if first else (carry,)), w, after)


def wave_tables(rows):
    window = 2 * rows
    angle = np.pi / window * (2 * np.arange(rows)[:, None] + 1) * np.arange(window)[None, :]
    forward = np.concatenate([np.cos(angle), np.sin(angle)], axis=0)
    inverse = forward[:, rows:].T * (2.0 / window)

    def pair(matrix):
        exact = jnp.asarray(matrix, jnp.float32)
        high = jnp.asarray(np.asarray(matrix, ml_dtypes.bfloat16))
        low = jnp.asarray(np.asarray(matrix - np.asarray(matrix, ml_dtypes.bfloat16).astype(np.float64), ml_dtypes.bfloat16))
        return high, low

    high, low = pair(forward)
    inverse_high, inverse_low = pair(inverse)
    return jnp.concatenate([high, low], axis=0), jnp.concatenate([inverse_high, inverse_low], axis=0)


def spectrum_kernel(taps_ref, forward_ref, _, out_ref):
    taps = taps_ref.shape[1]
    both = lax.dot_general(
        forward_ref[:, :taps], taps_ref[...], (((1,), (1,)), ((), ())), preferred_element_type=jnp.float32
    )
    half = out_ref.shape[0]
    out_ref[...] = both[:half, :] + both[half:, :]


def spectrum(taps, forward, after):
    channels = taps.shape[0]
    tile = tile_of(channels, 256)
    window = forward.shape[1]
    return pl.pallas_call(
        spectrum_kernel,
        grid=(channels // tile,),
        in_specs=[
            pl.BlockSpec((tile, taps.shape[1]), lambda i: (i, 0)),
            pl.BlockSpec(forward.shape, lambda i: (0, 0)),
            pl.BlockSpec(memory_space=pl.ANY),
        ],
        out_specs=pl.BlockSpec((window, tile), lambda i: (0, i)),
        out_shape=jax.ShapeDtypeStruct((window, channels), jnp.float32),
        compiler_params=params(),
        name="spectrum",
    )(taps, forward, after)


def mix_kernel(slot, info_ref, *refs):
    q0, k0, v0, q1, k1, v1, pk0, pv0, pk1, pv1, scale_ref, before_ref, f_ref, forward_ref, inverse_ref, _, out_ref, window = refs
    rows = out_ref.shape[0]
    block = block_of(slot, info_ref[2])
    length = info_ref[3]
    work = (block >= 0) & (block < slot[2])

    def joined(a_ref, b_ref):
        return a_ref[...].astype(jnp.float32) + b_ref[...].astype(jnp.float32)

    def wide(ref):
        return jnp.concatenate([ref[...]] * (out_ref.shape[1] // lanes), axis=1)

    @pl.when(work)
    def _():
        row = lax.broadcasted_iota(jnp.int32, (rows, 1), 0)
        scale = wide(scale_ref)
        live = (row + block * rows < length).astype(jnp.float32)
        here = joined(k0, k1) * scale * (joined(v0, v1) * scale) * live
        window[rows:, :] = here.astype(jnp.bfloat16)

        @pl.when(block > 0)
        def _():
            scale = wide(before_ref)
            live = (row + (block - 1) * rows < length).astype(jnp.float32)
            before = joined(pk0, pk1) * scale * (joined(pv0, pv1) * scale) * live
            window[:rows, :] = before.astype(jnp.bfloat16)

        @pl.when(block == 0)
        def _():
            window[:rows, :] = jnp.zeros((rows, window.shape[1]), jnp.bfloat16)

        both = jnp.dot(forward_ref[...], window[...], preferred_element_type=jnp.float32)
        cosine = both[:rows, :] + both[2 * rows : 3 * rows, :]
        sine = both[rows : 2 * rows, :] + both[3 * rows :, :]
        f_cosine = f_ref[:rows, :]
        f_sine = f_ref[rows:, :]
        product = jnp.concatenate(
            [cosine * f_cosine - sine * f_sine, cosine * f_sine + sine * f_cosine], axis=0
        )
        high = product.astype(jnp.bfloat16)
        low = (product - high.astype(jnp.float32)).astype(jnp.bfloat16)
        back = jnp.dot(inverse_ref[...], high, preferred_element_type=jnp.float32)
        conv = back[:rows, :] + back[rows:, :]
        conv = conv + jnp.dot(inverse_ref[:rows, :], low, preferred_element_type=jnp.float32)
        out_ref[...] = (joined(q0, q1) * scale * conv * live).astype(jnp.bfloat16)

    @pl.when(jnp.logical_not(work))
    def _():
        out_ref[...] = jnp.zeros_like(out_ref)


def mix(slot, here, before, rows, waves, filter_waves, scales, info, after):
    own, got, at = here
    own_before, got_before, at_before = before
    channels = filter_waves.shape[1] // 2
    tile = tile_of(channels, 256)
    per = channels // tile

    def spec(at, stream):
        return pl.BlockSpec((rows, tile), lambda i, held: (at, stream * per + i))

    def scale(offset):
        def index(i, held):
            return (jnp.clip(block_of(slot, held[2]) - offset, 0, slot[2] - 1), 0)

        return pl.BlockSpec((rows, lanes), index)

    whole = [pl.BlockSpec(wave.shape, lambda i, held: (0, 0)) for wave in waves]
    return pl.pallas_call(
        functools.partial(mix_kernel, slot),
        grid_spec=pltpu.PrefetchScalarGridSpec(
            num_scalar_prefetch=1,
            grid=(per,),
            in_specs=[spec(at, 0), spec(at, 1), spec(at, 2)] * 2
            + [spec(at_before, 1), spec(at_before, 2)] * 2
            + [scale(0), scale(1), pl.BlockSpec((2 * rows, tile), lambda i, held: (0, held[0] * per + i))]
            + whole
            + [pl.BlockSpec(memory_space=pl.ANY)],
            out_specs=pl.BlockSpec((rows, tile), lambda i, held: (0, i)),
            scratch_shapes=[pltpu.VMEM((2 * rows, tile), jnp.bfloat16)],
        ),
        out_shape=jax.ShapeDtypeStruct((rows, channels), jnp.bfloat16),
        compiler_params=params(),
        cost_estimate=pl.CostEstimate(
            flops=16 * rows * rows * channels, bytes_accessed=32 * rows * channels, transcendentals=0
        ),
        name="mix",
    )(
        info, own, own, own, got, got, got, own_before, own_before, got_before, got_before,
        scales, scales, filter_waves, *waves, after,
    )


def emit_kernel(slot, info_ref, mine_ref, theirs_ref, w_mine_ref, w_theirs_ref, _, *out_refs):
    block = block_of(slot, info_ref[2])
    work = (block >= 0) & (block < slot[2])
    chunk = out_refs[0].shape[0]

    @pl.when(work)
    def _():
        product = jnp.dot(mine_ref[...], w_mine_ref[...], preferred_element_type=jnp.float32)
        product = product + jnp.dot(theirs_ref[...], w_theirs_ref[...], preferred_element_type=jnp.float32)
        product = product.astype(jnp.bfloat16)
        for index, out_ref in enumerate(out_refs):
            out_ref[...] = product[index * chunk : (index + 1) * chunk, :]

    @pl.when(jnp.logical_not(work))
    def _():
        for out_ref in out_refs:
            out_ref[...] = jnp.zeros_like(out_ref)


def emit(slot, mine, theirs, w, info, after):
    rows, half = mine.shape
    width = w.shape[1]
    tile = tile_of(width, 1024)
    chunk = rows // halves
    whole = pl.BlockSpec((rows, half), lambda i, held: (0, 0))
    return pl.pallas_call(
        functools.partial(emit_kernel, slot),
        grid_spec=pltpu.PrefetchScalarGridSpec(
            num_scalar_prefetch=1,
            grid=(width // tile,),
            in_specs=[
                whole,
                whole,
                pl.BlockSpec((half, tile), lambda i, held: (held[0], i)),
                pl.BlockSpec((half, tile), lambda i, held: (held[1], i)),
                pl.BlockSpec(memory_space=pl.ANY),
            ],
            out_specs=[pl.BlockSpec((chunk, tile), lambda i, held: (0, i))] * halves,
        ),
        out_shape=[jax.ShapeDtypeStruct((chunk, width), jnp.bfloat16)] * halves,
        compiler_params=params(),
        cost_estimate=pl.CostEstimate(
            flops=4 * rows * half * width, bytes_accessed=4 * half * width, transcendentals=0
        ),
        name="emit",
    )(info, mine, theirs, w, w, after)


def finish_kernel(*refs):
    total = refs[0][...].astype(jnp.float32)
    for ref in refs[1:-1]:
        total = total + ref[...].astype(jnp.float32)
    refs[-1][...] = total.astype(jnp.bfloat16)


def finish(x, index, terms):
    chunk, width = terms[0].shape
    tile = tile_of(width, 1024)
    return pl.pallas_call(
        finish_kernel,
        grid=(width // tile,),
        in_specs=[pl.BlockSpec((chunk, tile), lambda i: (index, i))]
        + [pl.BlockSpec((chunk, tile), lambda i: (0, i))] * len(terms),
        out_specs=pl.BlockSpec((chunk, tile), lambda i: (0, i)),
        out_shape=jax.ShapeDtypeStruct((chunk, width), jnp.bfloat16),
        compiler_params=params(),
        cost_estimate=pl.CostEstimate(
            flops=chunk * width * len(terms), bytes_accessed=2 * chunk * width * (len(terms) + 2), transcendentals=0
        ),
        name="finish",
    )(x, *terms)


def added(*terms):
    total = terms[0].astype(jnp.float32)
    for term in terms[1:]:
        total = total + term.astype(jnp.float32)
    return total.astype(jnp.bfloat16)


def layer(spans, norm_gain, w_in, filters, w_out, prompt_len, needles):
    count = lax.axis_size("ctx")
    place = lax.axis_index("ctx")
    x_local = spans[0]
    rows, half_width = x_local.shape
    full_width = half_width * lax.axis_size("mp")
    weights = jnp.swapaxes(w_in[0], 0, 1)
    up = [(source, source + 1) for source in range(count - 1)]
    down = [(source + 1, source) for source in range(count - 1)]
    partner = [(0, 1), (1, 0)] if lax.axis_size("mp") == 2 else None

    far = count - 1
    order = [("d", 0)] + [(kind, k) for k in range(1, far) for kind in "du"] + [("m", far)]
    z = place.astype(jnp.int32)

    core = lax.axis_index("mp").astype(jnp.int32)
    info = jnp.concatenate([jnp.stack([core, 1 - core, z]), prompt_len])
    waves = wave_tables(rows)
    *pieces, squares = prepare(x_local, norm_gain)
    mine = (jnp.arange(count)[:, None] == z).astype(jnp.float32) * squares[:, 0][None, :]
    total = lax.psum(mine.reshape(-1), ("ctx", "mp"))
    scales = jnp.broadcast_to(lax.rsqrt(total / full_width + norm_eps)[:, None], (count * rows, lanes))
    gathered = {("d", 0): pieces, ("u", 0): pieces}
    for k in range(1, count):
        gathered["u", k] = []
        gathered["d", k] = []
        for i in range(halves):
            value = lax.ppermute(gathered["u", k - 1][i], "ctx", [(a, b) for a, b in up if a >= k - 1])
            gathered["u", k].append(value)
            value = lax.ppermute(gathered["d", k - 1][i], "ctx", [(a, b) for a, b in down if a <= count - k])
            gathered["d", k].append(value)

    held = {}
    gated = {}
    sums = {}

    def combine(kind, k, after):
        before = ("u", k + 1) if kind == "u" or k == 0 else ("d", k - 1)
        mine = mix(
            (kind, k, count), held["d" if kind == "m" else kind, k], held[before],
            rows, waves, filter_waves, scales, info, after,
        )
        gated[kind, k] = (mine, lax.ppermute(mine, "mp", partner))
        return mine

    def spread(kind, k, after):
        sums[kind, k] = emit((kind, k, count), *gated[kind, k], w_out[0], info, after)
        return sums[kind, k][0]

    filter_waves = spectrum(filters[0], waves[0], scales)
    after = filter_waves
    for group in groups_of(count):
        name = group[0]
        layout = []
        inputs = [[] for _ in range(halves)]
        for k in group:
            merged = 2 * k >= count
            for kind in ("d",) if k == 0 else ("ud",) if merged else ("u", "d"):
                for way in kind:
                    held[way, k] = len(layout)
                    for i in range(halves):
                        inputs[i].append(gathered[way, k][i])
                layout.append(len(kind))
        carry = None
        for i in range(halves - 1 if name else 0):
            carry = project(inputs[i : i + 1], layout, weights, i, carry, None, info, after)
            after = carry
        inputs, part = (inputs[-1:], halves - 1) if name else (inputs, 0)
        theirs = project(inputs, layout, weights, part, carry, 1, info, after)
        got = lax.ppermute(theirs, "mp", partner)
        mine = project(inputs, layout, weights, part, carry, 0, info, theirs)
        after = mine
        for k in group:
            for way in "d" if k == 0 else "ud":
                held[way, k] = (mine, got, held[way, k])
        for kind, k in early_slots(count) if name == 1 else ():
            after = combine(kind, k, after)
        for kind, k in early_slots(count) if name == 1 else ():
            after = spread(kind, k, after)
    rest = [slot for slot in [("m", far)] + [(kind, k) for k in range(far - 1, 0, -1) for kind in "ud"] + [("d", 0)]]
    rest = [slot for slot in rest if slot not in sums]
    after = combine(*rest[0], after)
    for index, slot in enumerate(rest):
        if index + 1 < len(rest):
            after = combine(*rest[index + 1], after)
        after = spread(*slot, after)

    def reduce_step(values, pairs):
        moved = []
        for value in values:
            moved.append(lax.ppermute(value, "ctx", pairs))
        return moved

    terms = [sums["d", 0]]
    for k in range(far, 0, -1):
        to_up = [(a, b) for a, b in up if a + k <= far]
        to_down = [(a, b) for a, b in down if a >= k]
        if k == far and far != 2:
            arrived = [reduce_step(sums["m", far], to_up + to_down)] * 2
        else:
            from_up, from_down = ("m", "m") if k == far else ("d", "u")
            arrived = [reduce_step(sums[from_up, k], to_up), reduce_step(sums[from_down, k], to_down)]
        if k > 1:
            for kind, moved in zip("du", arrived):
                sums[kind, k - 1] = [added(a, b) for a, b in zip(sums[kind, k - 1], moved)]
        else:
            terms += arrived if far > 1 else arrived[:1]
    sections = lax.axis_size("section")
    turn = [(source, (source + 1) % sections) for source in range(sections)]
    advanced = []
    for i in range(halves):
        final = finish(x_local, i, [term[i] for term in terms])
        advanced.append(lax.ppermute(final, "section", turn))
    advanced = jnp.concatenate(advanced, axis=0)[None]

    row = jnp.arange(rows, dtype=jnp.int32)
    picked = [0.0, 0.0]
    for slot in order:
        one_hot = (needles[0][:, None] == (row + block_of(slot, z) * rows)[None, :]).astype(jnp.bfloat16)
        for index, part in enumerate(gated[slot]):
            picked[index] += jnp.dot(one_hot, part, preferred_element_type=jnp.float32)
    mine, theirs = [value.astype(jnp.bfloat16) for value in picked]
    lower = jnp.where(core == 0, mine, theirs)
    upper = jnp.where(core == 0, theirs, mine)
    return (advanced, jnp.concatenate([lower, upper], axis=1)[None])


def groups_of(count):
    return [[0], [1]] + [list(range(k, min(k + 2, count))) for k in range(2, count, 2)]


def early_slots(count):
    return [("d", 0), ("d", 1)] if count > 2 else []


def solution(mesh):
    return jax.shard_map(
        layer,
        mesh=mesh,
        in_specs=(
            P("section", ("groups", "ctx"), "mp"),
            P("section", "mp"),
            P("section", "mp", None, "ctx"),
            P("section", "ctx", None),
            P("section", "ctx", "mp"),
            P(("groups", "section")),
            P("section", "groups"),
        ),
        out_specs=(P("section", ("groups", "ctx"), "mp"), P("section", "groups", "ctx")),
        check_vma=False,
    )
```

```python
import functools

import jax
import jax.numpy as jnp
import ml_dtypes
import numpy as np
from jax import lax
from jax.experimental import pallas as pl
from jax.experimental.pallas import tpu as pltpu
from jax.sharding import PartitionSpec as P


norm_eps = 1e-06
lanes = 128
sublanes = 8
stat_rows = 16
halves = 2
mebibyte = 1024 * 1024


def tile_of(extent, most):
    tile = min(extent, most)
    while extent % tile:
        tile //= 2
    return tile


def block_of(slot, z):
    kind, k = slot[:2]
    below = z - k
    return z + k if kind == "d" else jnp.where(z == 0, k, below) if kind == "m" else below


def params(grant=8):
    return pltpu.CompilerParams(vmem_limit_bytes=grant * mebibyte)


def vmem(count):
    return [pl.BlockSpec(memory_space=pltpu.VMEM)] * count


def hbm():
    return [pl.BlockSpec(memory_space=pltpu.HBM)]


def order_only():
    return [pl.BlockSpec(memory_space=pl.ANY)]


def smem():
    return [pl.BlockSpec(memory_space=pltpu.SMEM)]


def first_half_kernel(x_ref, gain_ref, out_ref, squares_ref):
    half = out_ref.shape[1]
    rows = x_ref.shape[0]
    x = x_ref[:, :half].astype(jnp.float32)
    out_ref[...] = (x * gain_ref[:, :half]).astype(jnp.bfloat16)
    other = x_ref[:, half:].astype(jnp.float32)
    total = jnp.sum(x * x, axis=1, keepdims=True) + jnp.sum(other * other, axis=1, keepdims=True)
    squares_ref[...] = jnp.transpose(jnp.broadcast_to(total, (rows, lanes)))[:sublanes, :]


def first_half(x, gain):
    rows, width = x.shape
    return pl.pallas_call(
        first_half_kernel,
        in_specs=vmem(2),
        out_specs=vmem(2),
        out_shape=[
            jax.ShapeDtypeStruct((rows, width // 2), jnp.bfloat16),
            jax.ShapeDtypeStruct((sublanes, rows), jnp.float32),
        ],
        compiler_params=params(),
        name="first_half",
    )(x, gain)


def second_half_kernel(x_ref, gain_ref, mine_ref, theirs_ref, out_ref):
    rows, width = x_ref.shape
    for tile in range(width // 2 // lanes):
        place = slice(width // 2 + tile * lanes, width // 2 + (tile + 1) * lanes)
        x = x_ref[:, place].astype(jnp.float32)
        out_ref[tile * rows : (tile + 1) * rows, :] = (x * gain_ref[:, place]).astype(jnp.bfloat16)
    total = mine_ref[:1, :] + theirs_ref[:1, :]
    high = total.astype(jnp.bfloat16).astype(jnp.float32)
    row = lax.broadcasted_iota(jnp.int32, (stat_rows, rows), 0)
    both = jnp.where(row == 0, high, jnp.where(row == 1, total - high, 0.0))
    out_ref[rows * (width // 2 // lanes) :, :] = both.astype(jnp.bfloat16)


def second_half(x, gain, mine, theirs):
    rows, width = x.shape
    return pl.pallas_call(
        second_half_kernel,
        in_specs=vmem(4),
        out_specs=vmem(1)[0],
        out_shape=jax.ShapeDtypeStruct((rows * (width // 2 // lanes) + stat_rows, lanes), jnp.bfloat16),
        compiler_params=params(),
        name="second_half",
    )(x, gain, mine, theirs)


def project_kernel(layout, which, side, first, info_ref, *refs):
    x_refs = refs[: sum(layout) * len(which)]
    refs = refs[sum(layout) * len(which) :]
    carry_ref = None if first else refs[0]
    w_hbm, _, out_ref, joined, w_ref, arrived = refs if first else refs[1:]
    rows = joined.shape[0] // len(layout)
    depth = joined.shape[1] // len(which)
    streams, _, channels = w_hbm.shape
    half = channels // 2
    source = 0
    deep = slice(which[0] * depth, which[0] * depth + joined.shape[1])
    steps = 1 if side is not None else 2

    def weights(index):
        stream = index if steps == 1 else lax.div(index, 2)
        offset = info_ref[side] * half if steps == 1 else lax.rem(index, 2) * half
        place = pl.ds(pl.multiple_of(offset, half), half)
        return pltpu.make_async_copy(w_hbm.at[stream, deep, place], w_ref.at[index], arrived.at[index])

    @pl.loop(0, streams * steps)
    def _(index):
        weights(index).start()

    def total(group, place):
        x = x_refs[group[0]][place]
        for other in group[1:]:
            x = x + x_refs[other][place]
        return x

    for part, stacked in enumerate(which):
        for index, inputs in enumerate(layout):
            group = range(source, source + inputs)
            source += inputs
            here = slice(index * rows, (index + 1) * rows)
            if stacked:
                for tile in range(depth // lanes):
                    column = part * depth + tile * lanes
                    joined[here, column : column + lanes] = total(
                        group, (slice(tile * rows, (tile + 1) * rows), slice(None))
                    )
            else:
                joined[here, part * depth : (part + 1) * depth] = total(group, (slice(None), slice(None)))

    @pl.loop(0, streams * steps)
    def _(index):
        weights(index).wait()
        value = jnp.dot(joined[...], w_ref[index], preferred_element_type=jnp.float32)
        if not first:
            offset = index * channels + info_ref[side] * half
            value = value + carry_ref[:, pl.ds(pl.multiple_of(offset, half), half)]
        out_ref[:, pl.ds(pl.multiple_of(index * half, half), half)] = value.astype(out_ref.dtype)


def project(pieces, layout, which, rows, w, carry, side, info, after):
    streams, deep, channels = w.shape
    total_rows = rows * len(layout)
    depth = deep // 2 * len(which)
    final = side is not None
    width = streams * channels // (2 if final else 1)
    flat = [piece for group in pieces for piece in group]
    carried = () if carry is None else (carry,)
    return pl.pallas_call(
        functools.partial(project_kernel, layout, which, side, carry is None),
        in_specs=smem() + vmem(len(flat) + len(carried)) + hbm() + order_only(),
        out_specs=vmem(1)[0],
        out_shape=jax.ShapeDtypeStruct((total_rows, width), jnp.bfloat16 if final else jnp.float32),
        scratch_shapes=[
            pltpu.VMEM((total_rows, depth), jnp.bfloat16),
            pltpu.VMEM((width // (channels // 2), depth, channels // 2), jnp.bfloat16),
            pltpu.SemaphoreType.DMA((width // (channels // 2),)),
        ],
        compiler_params=params(46),
        cost_estimate=pl.CostEstimate(
            flops=2 * total_rows * depth * width, bytes_accessed=2 * depth * width, transcendentals=0
        ),
        name="project",
    )(info, *flat, *carried, w, after)


def wave_tables(rows):
    window = 2 * rows
    angle = np.pi / window * (2 * np.arange(rows)[:, None] + 1) * np.arange(window)[None, :]
    forward = np.concatenate([np.cos(angle), np.sin(angle)], axis=0)
    inverse = forward[:, rows:].T * (2.0 / window)

    def pair(matrix):
        exact = jnp.asarray(matrix, jnp.float32)
        high = jnp.asarray(np.asarray(matrix, ml_dtypes.bfloat16))
        low = jnp.asarray(np.asarray(matrix - np.asarray(matrix, ml_dtypes.bfloat16).astype(np.float64), ml_dtypes.bfloat16))
        return high, low

    high, low = pair(forward)
    inverse_high, inverse_low = pair(inverse)
    return jnp.concatenate([high, low], axis=0), jnp.concatenate([inverse_high, inverse_low], axis=0)


def spectrum_kernel(taps_ref, forward_ref, _, out_ref):
    taps = taps_ref.shape[1]
    both = lax.dot_general(
        forward_ref[:, :taps], taps_ref[...], (((1,), (1,)), ((), ())), preferred_element_type=jnp.float32
    )
    half = out_ref.shape[0]
    out_ref[...] = both[:half, :] + both[half:, :]


def spectrum(taps, forward, after):
    return pl.pallas_call(
        spectrum_kernel,
        in_specs=vmem(2) + order_only(),
        out_specs=vmem(1)[0],
        out_shape=jax.ShapeDtypeStruct((forward.shape[1], taps.shape[0]), jnp.float32),
        compiler_params=params(),
        name="spectrum",
    )(taps, forward, after)


def mix_kernel(slot, at, before_at, stats, full_width, info_ref, *refs):
    own, got, own_before, got_before, *refs = refs
    stat_refs = refs[: stats[0]]
    before_refs = refs[stats[0] : stats[0] + stats[1]]
    f_ref, forward_ref, inverse_ref, _, out_ref, window = refs[stats[0] + stats[1] :]
    rows, half = out_ref.shape
    block = block_of(slot, info_ref[2])
    length = info_ref[3]
    work = (block >= 0) & (block < slot[2])
    tile = tile_of(half, 256)

    def scale_of(stat_refs):
        total = jnp.zeros((1, rows), jnp.float32)
        for ref in stat_refs:
            last = ref.shape[0] - stat_rows
            pair = ref[last:, :].astype(jnp.float32)
            total = total + pair[:1, :] + pair[1:2, :]
        total = jnp.transpose(jnp.broadcast_to(total, (lanes, rows)))
        scale = lax.rsqrt(total / full_width + norm_eps)
        return jnp.concatenate([scale] * (tile // lanes), axis=1)

    def joined(a_ref, b_ref, at, stream, column):
        place = (slice(at * rows, (at + 1) * rows), slice(stream * half + column, stream * half + column + tile))
        return a_ref[place].astype(jnp.float32) + b_ref[place].astype(jnp.float32)

    @pl.when(work)
    def _():
        row = lax.broadcasted_iota(jnp.int32, (rows, 1), 0)
        scale = scale_of(stat_refs)
        live = (row + block * rows < length).astype(jnp.float32)
        for column in range(0, half, tile):
            here = joined(own, got, at, 1, column) * scale * (joined(own, got, at, 2, column) * scale) * live
            window[rows:, column : column + tile] = here.astype(jnp.bfloat16)

        @pl.when(block > 0)
        def _():
            scale = scale_of(before_refs)
            live = (row + (block - 1) * rows < length).astype(jnp.float32)
            for column in range(0, half, tile):
                key = joined(own_before, got_before, before_at, 1, column) * scale
                value = joined(own_before, got_before, before_at, 2, column) * scale
                window[:rows, column : column + tile] = (key * value * live).astype(jnp.bfloat16)

        @pl.when(block == 0)
        def _():
            window[:rows, :] = jnp.zeros((rows, half), jnp.bfloat16)

        for column in range(0, half, tile):
            place = slice(column, column + tile)
            both = jnp.dot(forward_ref[...], window[:, place], preferred_element_type=jnp.float32)
            cosine = both[:rows, :] + both[2 * rows : 3 * rows, :]
            sine = both[rows : 2 * rows, :] + both[3 * rows :, :]
            channel = pl.ds(pl.multiple_of(info_ref[0] * half + column, tile), tile)
            f_cosine = f_ref[:rows, channel]
            f_sine = f_ref[rows:, channel]
            product = jnp.concatenate(
                [cosine * f_cosine - sine * f_sine, cosine * f_sine + sine * f_cosine], axis=0
            )
            high = product.astype(jnp.bfloat16)
            low = (product - high.astype(jnp.float32)).astype(jnp.bfloat16)
            back = jnp.dot(inverse_ref[...], high, preferred_element_type=jnp.float32)
            conv = back[:rows, :] + back[rows:, :]
            conv = conv + jnp.dot(inverse_ref[:rows, :], low, preferred_element_type=jnp.float32)
            out_ref[:, place] = (joined(own, got, at, 0, column) * scale * conv * live).astype(jnp.bfloat16)

    @pl.when(jnp.logical_not(work))
    def _():
        out_ref[...] = jnp.zeros_like(out_ref)


def mix(slot, here, before, stats, before_stats, rows, waves, filter_waves, full_width, info, after):
    own, got, at = here
    own_before, got_before, before_at = before
    half = filter_waves.shape[1] // 2
    counts = (len(stats), len(before_stats))
    return pl.pallas_call(
        functools.partial(mix_kernel, slot, at, before_at, counts, full_width),
        in_specs=smem() + vmem(4 + sum(counts) + 3) + order_only(),
        out_specs=vmem(1)[0],
        out_shape=jax.ShapeDtypeStruct((rows, half), jnp.bfloat16),
        scratch_shapes=[pltpu.VMEM((2 * rows, half), jnp.bfloat16)],
        compiler_params=params(),
        cost_estimate=pl.CostEstimate(
            flops=16 * rows * rows * half, bytes_accessed=32 * rows * half, transcendentals=0
        ),
        name="mix",
    )(info, own, got, own_before, got_before, *stats, *before_stats, filter_waves, *waves, after)


def emit_kernel(slot, info_ref, mine_ref, theirs_ref, w_hbm, _, *refs):
    *out_refs, w_ref, arrived = refs
    block = block_of(slot, info_ref[2])
    work = (block >= 0) & (block < slot[2])
    chunk, width = out_refs[0].shape
    half = mine_ref.shape[1]
    tile = tile_of(width, 512)

    @pl.when(work)
    def _():
        mine = pl.ds(pl.multiple_of(info_ref[0] * half, half), half)
        theirs = pl.ds(pl.multiple_of(info_ref[1] * half, half), half)

        def weights(index):
            place = pl.ds(pl.multiple_of(index * tile, tile), tile)
            return pltpu.make_async_copy(w_hbm.at[:, place], w_ref.at[index], arrived.at[index])

        @pl.loop(0, width // tile)
        def _(index):
            weights(index).start()

        @pl.loop(0, width // tile)
        def _(index):
            weights(index).wait()
            product = jnp.dot(mine_ref[...], w_ref[index, mine, :], preferred_element_type=jnp.float32)
            product = product + jnp.dot(theirs_ref[...], w_ref[index, theirs, :], preferred_element_type=jnp.float32)
            product = product.astype(jnp.bfloat16)
            place = pl.ds(pl.multiple_of(index * tile, tile), tile)
            for part, out_ref in enumerate(out_refs):
                out_ref[:, place] = product[part * chunk : (part + 1) * chunk, :]

    @pl.when(jnp.logical_not(work))
    def _():
        for out_ref in out_refs:
            out_ref[...] = jnp.zeros_like(out_ref)


def emit(slot, mine, theirs, w, info, after):
    rows, half = mine.shape
    width = w.shape[1]
    chunk = rows // halves
    return pl.pallas_call(
        functools.partial(emit_kernel, slot),
        in_specs=smem() + vmem(2) + hbm() + order_only(),
        out_specs=vmem(halves),
        out_shape=[jax.ShapeDtypeStruct((chunk, width), jnp.bfloat16)] * halves,
        scratch_shapes=[
            pltpu.VMEM((width // tile_of(width, 512), w.shape[0], tile_of(width, 512)), jnp.bfloat16),
            pltpu.SemaphoreType.DMA((width // tile_of(width, 512),)),
        ],
        compiler_params=params(50),
        cost_estimate=pl.CostEstimate(
            flops=4 * rows * half * width, bytes_accessed=4 * half * width, transcendentals=0
        ),
        name="emit",
    )(info, mine, theirs, w, after)


def finish_kernel(index, x_ref, *refs):
    chunk = refs[-1].shape[0]
    total = x_ref[index * chunk : (index + 1) * chunk, :].astype(jnp.float32)
    for ref in refs[:-1]:
        total = total + ref[...].astype(jnp.float32)
    refs[-1][...] = total.astype(jnp.bfloat16)


def finish(x, index, terms):
    chunk, width = terms[0].shape
    return pl.pallas_call(
        functools.partial(finish_kernel, index),
        in_specs=vmem(1 + len(terms)),
        out_specs=vmem(1)[0],
        out_shape=jax.ShapeDtypeStruct((chunk, width), jnp.bfloat16),
        compiler_params=params(),
        cost_estimate=pl.CostEstimate(
            flops=chunk * width * len(terms), bytes_accessed=2 * chunk * width * (len(terms) + 2), transcendentals=0
        ),
        name="finish",
    )(x, *terms)


def added(*terms):
    total = terms[0].astype(jnp.float32)
    for term in terms[1:]:
        total = total + term.astype(jnp.float32)
    return total.astype(jnp.bfloat16)


def layer(spans, norm_gain, w_in, filters, w_out, prompt_len, needles):
    count = lax.axis_size("ctx")
    place = lax.axis_index("ctx")
    x_local = spans[0]
    rows, half_width = x_local.shape
    full_width = half_width * lax.axis_size("mp")
    weights = jnp.swapaxes(w_in[0], 0, 1)
    up = [(source, source + 1) for source in range(count - 1)]
    down = [(source + 1, source) for source in range(count - 1)]
    partner = [(0, 1), (1, 0)] if lax.axis_size("mp") == 2 else None

    far = count - 1
    order = [("d", 0)] + [(kind, k) for k in range(1, far) for kind in "du"] + [("m", far)]
    z = place.astype(jnp.int32)

    core = lax.axis_index("mp").astype(jnp.int32)
    info = jnp.concatenate([jnp.stack([core, 1 - core, z]), prompt_len])
    waves = wave_tables(rows)
    leading, squares = first_half(x_local, norm_gain)
    other_squares = lax.ppermute(squares, "mp", partner)
    pieces = [leading, second_half(x_local, norm_gain, squares, other_squares)]
    gathered = {("d", 0): pieces, ("u", 0): pieces}
    for k in range(1, count):
        gathered["u", k] = []
        gathered["d", k] = []
        for i in range(halves):
            value = lax.ppermute(gathered["u", k - 1][i], "ctx", [(a, b) for a, b in up if a >= k - 1])
            gathered["u", k].append(value)
            value = lax.ppermute(gathered["d", k - 1][i], "ctx", [(a, b) for a, b in down if a <= count - k])
            gathered["d", k].append(value)

    held = {}
    gated = {}
    sums = {}

    def stats_of(kind, k):
        if 2 * k >= count:
            return [gathered["u", k][-1], gathered["d", k][-1]]
        return [gathered["d" if kind == "m" else kind, k][-1]]

    def combine(kind, k, after):
        before = ("u", k + 1) if kind == "u" or k == 0 else ("d", k - 1)
        mine = mix(
            (kind, k, count), held["d" if kind == "m" else kind, k], held[before],
            stats_of(kind, k), stats_of(*before), rows, waves, filter_waves, full_width, info, after,
        )
        gated[kind, k] = (mine, lax.ppermute(mine, "mp", partner))
        return mine

    def spread(kind, k, after):
        sums[kind, k] = emit((kind, k, count), *gated[kind, k], w_out[0], info, after)
        return sums[kind, k][0]

    filter_waves = spectrum(filters[0], waves[0], pieces[1])
    after = filter_waves
    for group in groups_of(count):
        name = group[0]
        layout = []
        inputs = [[] for _ in range(halves)]
        for k in group:
            merged = 2 * k >= count
            for kind in ("d",) if k == 0 else ("ud",) if merged else ("u", "d"):
                for way in kind:
                    held[way, k] = len(layout)
                    for i in range(halves):
                        inputs[i].append(gathered[way, k][i])
                layout.append(len(kind))
        carry = None
        for i in range(halves - 1 if name else 0):
            carry = project(inputs[i : i + 1], layout, (i,), rows, weights, carry, None, info, after)
            after = carry
        inputs, which = (inputs[-1:], (1,)) if name else (inputs, (0, 1))
        theirs = project(inputs, layout, which, rows, weights, carry, 1, info, after)
        got = lax.ppermute(theirs, "mp", partner)
        mine = project(inputs, layout, which, rows, weights, carry, 0, info, theirs)
        after = mine
        for k in group:
            for way in "d" if k == 0 else "ud":
                held[way, k] = (mine, got, held[way, k])
        for kind, k in early_slots(count) if name == 1 else ():
            after = combine(kind, k, after)
        for kind, k in early_slots(count) if name == 1 else ():
            after = spread(kind, k, after)
    rest = [slot for slot in [("m", far)] + [(kind, k) for k in range(far - 1, 0, -1) for kind in "ud"] + [("d", 0)]]
    rest = [slot for slot in rest if slot not in sums]
    after = combine(*rest[0], after)
    for index, slot in enumerate(rest):
        if index + 1 < len(rest):
            after = combine(*rest[index + 1], after)
        after = spread(*slot, after)

    def reduce_step(values, pairs):
        moved = []
        for value in values:
            moved.append(lax.ppermute(value, "ctx", pairs))
        return moved

    terms = [sums["d", 0]]
    for k in range(far, 0, -1):
        to_up = [(a, b) for a, b in up if a + k <= far]
        to_down = [(a, b) for a, b in down if a >= k]
        if k == far and far != 2:
            arrived = [reduce_step(sums["m", far], to_up + to_down)] * 2
        else:
            from_up, from_down = ("m", "m") if k == far else ("d", "u")
            arrived = [reduce_step(sums[from_up, k], to_up), reduce_step(sums[from_down, k], to_down)]
        if k > 1:
            for kind, moved in zip("du", arrived):
                sums[kind, k - 1] = [added(a, b) for a, b in zip(sums[kind, k - 1], moved)]
        else:
            terms += arrived if far > 1 else arrived[:1]
    sections = lax.axis_size("section")
    turn = [(source, (source + 1) % sections) for source in range(sections)]
    advanced = []
    for i in range(halves):
        final = finish(x_local, i, [term[i] for term in terms])
        advanced.append(lax.ppermute(final, "section", turn))
    advanced = jnp.concatenate(advanced, axis=0)[None]

    row = jnp.arange(rows, dtype=jnp.int32)
    picked = [0.0, 0.0]
    for slot in order:
        one_hot = (needles[0][:, None] == (row + block_of(slot, z) * rows)[None, :]).astype(jnp.bfloat16)
        for index, part in enumerate(gated[slot]):
            picked[index] += jnp.dot(one_hot, part, preferred_element_type=jnp.float32)
    mine, theirs = [value.astype(jnp.bfloat16) for value in picked]
    lower = jnp.where(core == 0, mine, theirs)
    upper = jnp.where(core == 0, theirs, mine)
    return (advanced, jnp.concatenate([lower, upper], axis=1)[None])


def groups_of(count):
    return [[0], [1]] + [list(range(k, min(k + 2, count))) for k in range(2, count, 2)]


def early_slots(count):
    return [("d", 0), ("d", 1)] if count > 2 else []


def solution(mesh):
    return jax.shard_map(
        layer,
        mesh=mesh,
        in_specs=(
            P("section", ("groups", "ctx"), "mp"),
            P("section", "mp"),
            P("section", "mp", None, "ctx"),
            P("section", "ctx", None),
            P("section", "ctx", "mp"),
            P(("groups", "section")),
            P("section", "groups"),
        ),
        out_specs=(P("section", ("groups", "ctx"), "mp"), P("section", "groups", "ctx")),
        check_vma=False,
    )
```

```python
import functools

import jax
import jax.numpy as jnp
import ml_dtypes
import numpy as np
from jax import lax
from jax.experimental import pallas as pl
from jax.experimental.pallas import tpu as pltpu
from jax.sharding import PartitionSpec as P


norm_eps = 1e-06
lanes = 128
stat_rows = 16
halves = 2
mebibyte = 1024 * 1024


def tile_of(extent, most):
    tile = min(extent, most)
    while extent % tile:
        tile //= 2
    return tile


def block_of(slot, z):
    kind, k = slot[:2]
    below = z - k
    return z + k if kind == "d" else jnp.where(z == 0, k, below) if kind == "m" else below


def params(grant=8):
    return pltpu.CompilerParams(vmem_limit_bytes=grant * mebibyte)


def vmem(count):
    return [pl.BlockSpec(memory_space=pltpu.VMEM)] * count


def hbm():
    return [pl.BlockSpec(memory_space=pltpu.HBM)]


def order_only():
    return [pl.BlockSpec(memory_space=pl.ANY)]


def smem():
    return [pl.BlockSpec(memory_space=pltpu.SMEM)]


def prepare_kernel(x_hbm, gain_hbm, out_ref, x_ref, gain_ref, arrived):
    copies = [
        pltpu.make_async_copy(x_hbm, x_ref, arrived.at[0]),
        pltpu.make_async_copy(gain_hbm, gain_ref, arrived.at[1]),
    ]
    for copy in copies:
        copy.start()
    for copy in copies:
        copy.wait()
    rows, width = x_ref.shape
    total = jnp.zeros((rows, lanes), jnp.float32)
    for tile in range(width // lanes):
        place = slice(tile * lanes, (tile + 1) * lanes)
        x = x_ref[:, place].astype(jnp.float32)
        out_ref[tile * rows : (tile + 1) * rows, :] = (x * gain_ref[:, place]).astype(jnp.bfloat16)
        total = total + x * x
    total = jnp.transpose(jnp.broadcast_to(jnp.sum(total, axis=1, keepdims=True), (rows, lanes)))
    total = jnp.broadcast_to(total[:1, :], (stat_rows, rows))
    high = total.astype(jnp.bfloat16).astype(jnp.float32)
    row = lax.broadcasted_iota(jnp.int32, (stat_rows, rows), 0)
    both = jnp.where(row == 0, high, jnp.where(row == 1, total - high, 0.0))
    out_ref[rows * (width // lanes) :, :] = both.astype(jnp.bfloat16)


def prepare(x, gain):
    rows, width = x.shape
    return pl.pallas_call(
        prepare_kernel,
        in_specs=hbm() * 2,
        out_specs=vmem(1)[0],
        out_shape=jax.ShapeDtypeStruct((rows * (width // lanes) + stat_rows, lanes), jnp.bfloat16),
        scratch_shapes=[
            pltpu.VMEM(x.shape, x.dtype),
            pltpu.VMEM(gain.shape, gain.dtype),
            pltpu.SemaphoreType.DMA((2,)),
        ],
        compiler_params=params(),
        name="prepare",
    )(x, gain)


def project_kernel(layout, side, info_ref, *refs):
    x_refs = refs[: sum(layout)]
    w_hbm, _, out_ref, joined, w_ref, arrived = refs[sum(layout) :]
    depth = joined.shape[1]
    rows = joined.shape[0] // len(layout)
    streams, _, channels = w_hbm.shape
    half = channels // 2

    def weights(stream):
        place = pl.ds(pl.multiple_of(info_ref[side] * half, half), half)
        return pltpu.make_async_copy(w_hbm.at[stream, :, place], w_ref.at[stream], arrived.at[stream])

    @pl.loop(0, streams)
    def _(stream):
        weights(stream).start()

    source = 0
    for index, inputs in enumerate(layout):
        group = x_refs[source : source + inputs]
        source += inputs

        def total(place):
            x = group[0][place, :]
            for other in group[1:]:
                x = x + other[place, :]
            return x

        here = slice(index * rows, (index + 1) * rows)
        for tile in range(depth // lanes):
            joined[here, tile * lanes : (tile + 1) * lanes] = total(slice(tile * rows, (tile + 1) * rows))
        below = joined.shape[0] + index * stat_rows
        last = rows * (depth // lanes)
        out_ref[below : below + stat_rows, :lanes] = total(slice(last, last + stat_rows))

    @pl.loop(0, streams)
    def _(stream):
        weights(stream).wait()
        value = jnp.dot(joined[...], w_ref[stream], preferred_element_type=jnp.float32)
        place = pl.ds(pl.multiple_of(stream * half, half), half)
        out_ref[: joined.shape[0], place] = value.astype(out_ref.dtype)


def project(pieces, layout, rows, w, side, info, after):
    streams, depth, channels = w.shape
    total_rows = rows * len(layout)
    half = channels // 2
    return pl.pallas_call(
        functools.partial(project_kernel, layout, side),
        in_specs=smem() + vmem(len(pieces)) + hbm() + order_only(),
        out_specs=vmem(1)[0],
        out_shape=jax.ShapeDtypeStruct((total_rows + stat_rows * len(layout), streams * half), jnp.bfloat16),
        scratch_shapes=[
            pltpu.VMEM((total_rows, depth), jnp.bfloat16),
            pltpu.VMEM((streams, depth, half), jnp.bfloat16),
            pltpu.SemaphoreType.DMA((streams,)),
        ],
        compiler_params=params(46),
        cost_estimate=pl.CostEstimate(
            flops=2 * total_rows * depth * streams * half,
            bytes_accessed=2 * depth * streams * half,
            transcendentals=0,
        ),
        name="project",
    )(info, *pieces, w, after)


def wave_tables(rows):
    window = 2 * rows
    angle = np.pi / window * (2 * np.arange(rows)[:, None] + 1) * np.arange(window)[None, :]
    forward = np.concatenate([np.cos(angle), np.sin(angle)], axis=0)
    inverse = forward[:, rows:].T * (2.0 / window)

    def pair(matrix):
        exact = jnp.asarray(matrix, jnp.float32)
        high = jnp.asarray(np.asarray(matrix, ml_dtypes.bfloat16))
        low = jnp.asarray(np.asarray(matrix - np.asarray(matrix, ml_dtypes.bfloat16).astype(np.float64), ml_dtypes.bfloat16))
        return high, low

    high, low = pair(forward)
    inverse_high, inverse_low = pair(inverse)
    return jnp.concatenate([high, low], axis=0), jnp.concatenate([inverse_high, inverse_low], axis=0)


def spectrum_kernel(taps_ref, forward_ref, _, out_ref):
    taps = taps_ref.shape[1]
    both = lax.dot_general(
        forward_ref[:, :taps], taps_ref[...], (((1,), (1,)), ((), ())), preferred_element_type=jnp.float32
    )
    half = out_ref.shape[0]
    out_ref[...] = both[:half, :] + both[half:, :]


def spectrum(taps, forward, after):
    return pl.pallas_call(
        spectrum_kernel,
        in_specs=vmem(2) + order_only(),
        out_specs=vmem(1)[0],
        out_shape=jax.ShapeDtypeStruct((forward.shape[1], taps.shape[0]), jnp.float32),
        compiler_params=params(),
        name="spectrum",
    )(taps, forward, after)


def mix_kernel(slot, at, before_at, full_width, info_ref, *refs):
    own, got, own_before, got_before, f_ref, forward_ref, inverse_ref, _, out_ref, window = refs
    rows, half = out_ref.shape
    block = block_of(slot, info_ref[2])
    length = info_ref[3]
    work = (block >= 0) & (block < slot[2])
    tile = tile_of(half, 256)

    def scale_of(own_ref, got_ref, at):
        blocks = own_ref.shape[0] // (rows + stat_rows)
        below = blocks * rows + at * stat_rows
        total = jnp.zeros((1, rows), jnp.float32)
        for ref in (own_ref, got_ref):
            pair = ref[below : below + stat_rows, :lanes].astype(jnp.float32)
            total = total + (pair[:1, :] + pair[1:2, :])
        total = jnp.transpose(jnp.broadcast_to(total, (lanes, rows)))
        scale = lax.rsqrt(total / full_width + norm_eps)
        return jnp.concatenate([scale] * (tile // lanes), axis=1)

    def joined(a_ref, b_ref, at, stream, column):
        place = (slice(at * rows, (at + 1) * rows), slice(stream * half + column, stream * half + column + tile))
        return a_ref[place].astype(jnp.float32) + b_ref[place].astype(jnp.float32)

    @pl.when(work)
    def _():
        row = lax.broadcasted_iota(jnp.int32, (rows, 1), 0)
        scale = scale_of(own, got, at)
        live = (row + block * rows < length).astype(jnp.float32)
        for column in range(0, half, tile):
            here = joined(own, got, at, 1, column) * scale * (joined(own, got, at, 2, column) * scale) * live
            window[rows:, column : column + tile] = here.astype(jnp.bfloat16)

        @pl.when(block > 0)
        def _():
            scale = scale_of(own_before, got_before, before_at)
            live = (row + (block - 1) * rows < length).astype(jnp.float32)
            for column in range(0, half, tile):
                key = joined(own_before, got_before, before_at, 1, column) * scale
                value = joined(own_before, got_before, before_at, 2, column) * scale
                window[:rows, column : column + tile] = (key * value * live).astype(jnp.bfloat16)

        @pl.when(block == 0)
        def _():
            window[:rows, :] = jnp.zeros((rows, half), jnp.bfloat16)

        for column in range(0, half, tile):
            place = slice(column, column + tile)
            both = jnp.dot(forward_ref[...], window[:, place], preferred_element_type=jnp.float32)
            cosine = both[:rows, :] + both[2 * rows : 3 * rows, :]
            sine = both[rows : 2 * rows, :] + both[3 * rows :, :]
            channel = pl.ds(pl.multiple_of(info_ref[0] * half + column, tile), tile)
            f_cosine = f_ref[:rows, channel]
            f_sine = f_ref[rows:, channel]
            product = jnp.concatenate(
                [cosine * f_cosine - sine * f_sine, cosine * f_sine + sine * f_cosine], axis=0
            )
            high = product.astype(jnp.bfloat16)
            low = (product - high.astype(jnp.float32)).astype(jnp.bfloat16)
            back = jnp.dot(inverse_ref[...], high, preferred_element_type=jnp.float32)
            conv = back[:rows, :] + back[rows:, :]
            conv = conv + jnp.dot(inverse_ref[:rows, :], low, preferred_element_type=jnp.float32)
            out_ref[:, place] = (joined(own, got, at, 0, column) * scale * conv * live).astype(jnp.bfloat16)

    @pl.when(jnp.logical_not(work))
    def _():
        out_ref[...] = jnp.zeros_like(out_ref)


def mix(slot, here, before, rows, waves, filter_waves, full_width, info, after):
    own, got, at = here
    own_before, got_before, before_at = before
    half = filter_waves.shape[1] // 2
    return pl.pallas_call(
        functools.partial(mix_kernel, slot, at, before_at, full_width),
        in_specs=smem() + vmem(7) + order_only(),
        out_specs=vmem(1)[0],
        out_shape=jax.ShapeDtypeStruct((rows, half), jnp.bfloat16),
        scratch_shapes=[pltpu.VMEM((2 * rows, half), jnp.bfloat16)],
        compiler_params=params(),
        cost_estimate=pl.CostEstimate(
            flops=16 * rows * rows * half, bytes_accessed=32 * rows * half, transcendentals=0
        ),
        name="mix",
    )(info, own, got, own_before, got_before, filter_waves, *waves, after)


def emit_kernel(slot, info_ref, mine_ref, theirs_ref, w_hbm, _, *refs):
    *out_refs, w_ref, arrived = refs
    block = block_of(slot, info_ref[2])
    work = (block >= 0) & (block < slot[2])
    chunk, width = out_refs[0].shape
    half = mine_ref.shape[1]
    tile = tile_of(width, 512)

    @pl.when(work)
    def _():
        mine = pl.ds(pl.multiple_of(info_ref[0] * half, half), half)
        theirs = pl.ds(pl.multiple_of(info_ref[1] * half, half), half)

        def weights(index):
            place = pl.ds(pl.multiple_of(index * tile, tile), tile)
            return pltpu.make_async_copy(w_hbm.at[:, place], w_ref.at[index], arrived.at[index])

        @pl.loop(0, width // tile)
        def _(index):
            weights(index).start()

        @pl.loop(0, width // tile)
        def _(index):
            weights(index).wait()
            product = jnp.dot(mine_ref[...], w_ref[index, mine, :], preferred_element_type=jnp.float32)
            product = product + jnp.dot(theirs_ref[...], w_ref[index, theirs, :], preferred_element_type=jnp.float32)
            product = product.astype(jnp.bfloat16)
            place = pl.ds(pl.multiple_of(index * tile, tile), tile)
            for part, out_ref in enumerate(out_refs):
                out_ref[:, place] = product[part * chunk : (part + 1) * chunk, :]

    @pl.when(jnp.logical_not(work))
    def _():
        for out_ref in out_refs:
            out_ref[...] = jnp.zeros_like(out_ref)


def emit(slot, mine, theirs, w, info, after):
    rows, half = mine.shape
    width = w.shape[1]
    chunk = rows // halves
    return pl.pallas_call(
        functools.partial(emit_kernel, slot),
        in_specs=smem() + vmem(2) + hbm() + order_only(),
        out_specs=vmem(halves),
        out_shape=[jax.ShapeDtypeStruct((chunk, width), jnp.bfloat16)] * halves,
        scratch_shapes=[
            pltpu.VMEM((width // tile_of(width, 512), w.shape[0], tile_of(width, 512)), jnp.bfloat16),
            pltpu.SemaphoreType.DMA((width // tile_of(width, 512),)),
        ],
        compiler_params=params(50),
        cost_estimate=pl.CostEstimate(
            flops=4 * rows * half * width, bytes_accessed=4 * half * width, transcendentals=0
        ),
        name="emit",
    )(info, mine, theirs, w, after)


def finish_kernel(index, x_ref, *refs):
    chunk = refs[-1].shape[0]
    total = x_ref[index * chunk : (index + 1) * chunk, :].astype(jnp.float32)
    for ref in refs[:-1]:
        total = total + ref[...].astype(jnp.float32)
    refs[-1][...] = total.astype(jnp.bfloat16)


def finish(x, index, terms):
    chunk, width = terms[0].shape
    return pl.pallas_call(
        functools.partial(finish_kernel, index),
        in_specs=vmem(1 + len(terms)),
        out_specs=vmem(1)[0],
        out_shape=jax.ShapeDtypeStruct((chunk, width), jnp.bfloat16),
        compiler_params=params(),
        cost_estimate=pl.CostEstimate(
            flops=chunk * width * len(terms), bytes_accessed=2 * chunk * width * (len(terms) + 2), transcendentals=0
        ),
        name="finish",
    )(x, *terms)


def readout_kernel(slots, info_ref, needle_ref, *refs):
    *refs, _, out_ref = refs
    rows, half = refs[0].shape
    row = lax.broadcasted_iota(jnp.int32, (rows, needle_ref.shape[1]), 0)
    totals = [jnp.zeros((needle_ref.shape[1], half), jnp.float32)] * 2
    for index, slot in enumerate(slots):
        chosen = row + block_of(slot, info_ref[2]) * rows == needle_ref[...]
        chosen = jnp.transpose(chosen.astype(jnp.float32)).astype(jnp.bfloat16)
        for side in range(2):
            part = refs[2 * index + side][...]
            totals[side] += jnp.dot(chosen, part, preferred_element_type=jnp.float32)
    for side in range(2):
        place = pl.ds(pl.multiple_of(info_ref[side] * half, half), half)
        out_ref[:, place] = totals[side].astype(jnp.bfloat16)


def readout(gated, needles, info, after):
    slots = list(gated)
    parts = [part for slot in slots for part in gated[slot]]
    half = parts[0].shape[1]
    return pl.pallas_call(
        functools.partial(readout_kernel, slots),
        in_specs=smem() + vmem(1 + len(parts)) + order_only(),
        out_specs=vmem(1)[0],
        out_shape=jax.ShapeDtypeStruct((needles.shape[1], 2 * half), jnp.bfloat16),
        compiler_params=params(),
        cost_estimate=pl.CostEstimate(
            flops=2 * needles.shape[1] * parts[0].shape[0] * half * len(parts), bytes_accessed=0, transcendentals=0
        ),
        name="readout",
    )(info, needles, *parts, after)


def added(*terms):
    total = terms[0].astype(jnp.float32)
    for term in terms[1:]:
        total = total + term.astype(jnp.float32)
    return total.astype(jnp.bfloat16)


def layer(spans, norm_gain, w_in, filters, w_out, prompt_len, needles):
    count = lax.axis_size("ctx")
    place = lax.axis_index("ctx")
    x_local = spans[0]
    rows, half_width = x_local.shape
    full_width = half_width * lax.axis_size("mp")
    weights = jnp.swapaxes(w_in[0], 0, 1)
    up = [(source, source + 1) for source in range(count - 1)]
    down = [(source + 1, source) for source in range(count - 1)]
    partner = [(0, 1), (1, 0)] if lax.axis_size("mp") == 2 else None

    far = count - 1
    z = place.astype(jnp.int32)

    core = lax.axis_index("mp").astype(jnp.int32)
    info = jnp.concatenate([jnp.stack([core, 1 - core, z]), prompt_len])
    waves = wave_tables(rows)
    piece = prepare(x_local, norm_gain)
    gathered = {("d", 0): piece, ("u", 0): piece}
    for k in range(1, count):
        to_up = [(a, b) for a, b in up if a >= k - 1]
        gathered["u", k] = lax.ppermute(gathered["u", k - 1], "ctx", to_up)
        to_down = [(a, b) for a, b in down if a <= count - k]
        gathered["d", k] = lax.ppermute(gathered["d", k - 1], "ctx", to_down)

    held = {}
    gated = {}
    sums = {}

    def combine(kind, k, after):
        before = ("u", k + 1) if kind == "u" or k == 0 else ("d", k - 1)
        mine = mix(
            (kind, k, count), held["d" if kind == "m" else kind, k], held[before],
            rows, waves, filter_waves, full_width, info, after,
        )
        gated[kind, k] = (mine, lax.ppermute(mine, "mp", partner))
        return mine

    def spread(kind, k, after):
        sums[kind, k] = emit((kind, k, count), *gated[kind, k], w_out[0], info, after)
        return sums[kind, k][0]

    filter_waves = spectrum(filters[0], waves[0], piece)
    after = filter_waves
    for k in range(count):
        kinds = ("d",) if k == 0 else ("ud",) if 2 * k >= count else ("u", "d")
        layout = [len(kind) for kind in kinds]
        inputs = [gathered[way, k] for kind in kinds for way in kind]
        theirs = project(inputs, layout, rows, weights, 1, info, after)
        got = lax.ppermute(theirs, "mp", partner)
        after = project(inputs, layout, rows, weights, 0, info, theirs)
        for index, kind in enumerate(kinds):
            for way in kind:
                held[way, k] = (after, got, index)
        if k == 0:
            held["u", 0] = held["d", 0]
        if count > 2 and k == 1:
            for slot in (("d", 0), ("d", 1)):
                after = combine(*slot, after)
        if count > 2 and k == 2:
            for slot in (("d", 0), ("d", 1)):
                after = spread(*slot, after)
    rest = [slot for slot in [("m", far)] + [(kind, k) for k in range(far - 1, 0, -1) for kind in "ud"] + [("d", 0)]]
    rest = [slot for slot in rest if slot not in sums]
    after = combine(*rest[0], after)
    for index, slot in enumerate(rest):
        if index + 1 < len(rest):
            after = combine(*rest[index + 1], after)
        after = spread(*slot, after)

    def reduce_step(values, pairs):
        moved = []
        for value in values:
            moved.append(lax.ppermute(value, "ctx", pairs))
        return moved

    terms = [sums["d", 0]]
    for k in range(far, 0, -1):
        to_up = [(a, b) for a, b in up if a + k <= far]
        to_down = [(a, b) for a, b in down if a >= k]
        if k == far and far != 2:
            arrived = [reduce_step(sums["m", far], to_up + to_down)] * 2
        else:
            from_up, from_down = ("m", "m") if k == far else ("d", "u")
            arrived = [reduce_step(sums[from_up, k], to_up), reduce_step(sums[from_down, k], to_down)]
        if k > 1:
            for kind, moved in zip("du", arrived):
                sums[kind, k - 1] = [added(a, b) for a, b in zip(sums[kind, k - 1], moved)]
        else:
            terms += arrived if far > 1 else arrived[:1]
    sections = lax.axis_size("section")
    turn = [(source, (source + 1) % sections) for source in range(sections)]
    advanced = []
    for i in range(halves):
        final = finish(x_local, i, [term[i] for term in terms])
        advanced.append(lax.ppermute(final, "section", turn))
    advanced = jnp.concatenate(advanced, axis=0)[None]

    picked = readout(gated, needles, info, after)
    return (advanced, picked[None])


def solution(mesh):
    return jax.shard_map(
        layer,
        mesh=mesh,
        in_specs=(
            P("section", ("groups", "ctx"), "mp"),
            P("section", "mp"),
            P("section", "mp", None, "ctx"),
            P("section", "ctx", None),
            P("section", "ctx", "mp"),
            P(("groups", "section")),
            P("section", "groups"),
        ),
        out_specs=(P("section", ("groups", "ctx"), "mp"), P("section", "groups", "ctx")),
        check_vma=False,
    )
```
